512 devices in a mesh: dp: 32 (over x, y), region: 16 (over z, core).
Axes of the slice: x: 4, y: 8, z: 8, core: 2. Of those that a mesh axis runs over, the one named last changes fastest.
Arguments:
- inputs: bfloat16 [32, 2, 4096, 256], P('dp', None, 'region'), may hold values from -6 to 6
- cotangent: bfloat16 [32, 2, 4096, 256], P('dp', None, 'region'), may hold values from -6 to 6
- w_filter: bfloat16 [2, 256, 256], replicated, may hold values from -0.25 to 0.25
- w_gate: bfloat16 [2, 256, 256], replicated, may hold values from -0.25 to 0.25
- w_mix: bfloat16 [2, 256, 256], replicated, may hold values from -0.25 to 0.25
- neighbours: int32 [32, 6], replicated, may hold values from 0 to 31, as said below
- adjacency: bfloat16 [32, 6, 128, 128], P('region'), may hold values from -0.21875 to 0.21875
Outputs:
- grad_inputs: bfloat16 [32, 2, 4096, 256], P('dp', None, 'region')
- grad_filter: float32 [2, 256, 256], replicated
- grad_gate: float32 [2, 256, 256], replicated
- grad_mix: float32 [2, 256, 256], replicated
The draws below stay inside these ranges and needn't reach their ends.
Inputs may be any that keep to these rules, and one draw needn't show every extreme that they name: `neighbours`: for every region r (tiles r * 2 to (r + 1) * 2 - 1), exactly 11 of the 12 entries of its tiles' lists name tiles of other regions, each of a different region, so at most 1 name tiles of any one other region; all other entries name tiles of region r.
All inputs are finite; a program needn't handle non-finite values.
Results may differ from the reference program's by a relative error of at most 0.0053.
Values may be sent and summed in bfloat16 or wider, within the bound.
A program may use at most 64 MiB of HBM per device.

```python
import math
import jax
import jax.numpy as jnp
from jax import lax

C = 256
TILE = 128
NB = 6
TL = 2
TILES_DEV = 2
TILES = 32
SITES = 4096
BATCH = 32


def draw_neighbours(key, part):
    regions = TILES // TILES_DEV
    entries = TILES_DEV * NB
    foreign = min(entries - 1, regions - 1)

    def one_region(region, region_key):
        other_key, entry_key, local_key = jax.random.split(region_key, 3)
        offsets = jnp.arange(1, regions, dtype=jnp.int32)
        spread = jax.random.permutation(other_key, regions - 1).astype(jnp.int32)
        scores = jnp.where(offsets == 1, 0, jnp.where(offsets == regions - 1, 1, jnp.where(offsets == regions // 2, 2, 3 + spread)))
        order_keys = jnp.argsort(scores, stable=True)
        chosen = offsets[order_keys][:foreign]
        others = (region + chosen) % regions
        owner_list = jnp.concatenate([others.astype(jnp.int32), jnp.full((entries - foreign,), region, jnp.int32)])
        order = jax.random.permutation(entry_key, entries)
        owners = owner_list[order]
        local_tile = jax.random.randint(local_key, (entries,), 0, TILES_DEV)
        return (owners * TILES_DEV + local_tile).astype(jnp.int32)
    region_keys = jax.random.split(jax.random.fold_in(key, 17), regions)
    table = jax.vmap(one_region)(jnp.arange(regions, dtype=jnp.int32), region_keys)
    return table.reshape(TILES, NB)


def shard_levels(stream_key, dims, cuts, least, top_value):
    level, own = 1.0, jax.random.fold_in(stream_key, 6)
    for axis_at, blocks in cuts:
        draws = jnp.exp(jax.random.uniform(jax.random.fold_in(own, axis_at), (blocks,), jnp.float32, least / len(cuts), top_value / len(cuts)))
        level = level * jnp.repeat(draws, dims[axis_at] // blocks).reshape([-1 if axis == axis_at else 1 for axis in range(len(dims))])
    return level


def bell_draw(rng, shape, deviation, limit, cuts=(), held_as=jnp.bfloat16):
    factor_of = shard_levels(rng, shape, cuts, -0.22, 0.18) if cuts else 1.0
    array = jax.random.normal(rng, shape, jnp.float32) * deviation * factor_of
    return jnp.minimum(jnp.maximum(array, -limit), limit).astype(held_as)


def setup_inputs(seed: int = 0) -> dict:
    splits = jax.random.split(jax.random.key(seed), 8)
    inputs = bell_draw(splits[0], (BATCH, TL, SITES, C), 1.0, 6.0, ((0, 32), (2, 16)))
    cotangent = bell_draw(splits[1], (BATCH, TL, SITES, C), 1.0, 6.0, ((0, 32), (2, 16)))
    w_filter = bell_draw(splits[2], (2, C, C), (2 * C) ** -0.5, 0.25)
    w_gate = bell_draw(splits[3], (2, C, C), (2 * C) ** -0.5, 0.25)
    w_mix = bell_draw(splits[4], (2, C, C), (2 * C) ** -0.5, 0.25)
    neighbours = draw_neighbours(jax.random.fold_in(splits[7], 71), 0)
    adjacency = bell_draw(splits[6], (TILES, NB, TILE, TILE), (NB * TILE) ** -0.5, 0.21875, ((0, 16),))
    return dict(inputs=inputs, cotangent=cotangent, w_filter=w_filter, w_gate=w_gate, w_mix=w_mix, neighbours=neighbours, adjacency=adjacency)


def reference(inputs, cotangent, w_filter, w_gate, w_mix, neighbours, adjacency):
    w_cat = jnp.concatenate([jnp.concatenate([w_filter[0], w_gate[0]], axis=1), jnp.concatenate([w_filter[1], w_gate[1]], axis=1)], axis=0)
    w_mixed = w_mix.reshape(2 * C, C)
    adj_wide = adjacency.astype(jnp.float32)
    flat_ids = neighbours.reshape(-1).astype(jnp.int32)

    def one_window(carry, pair):
        conv_sum, mix_sum = carry
        window_in, window_cot = pair
        previous = jnp.concatenate([jnp.zeros_like(window_in[:1]), window_in[:-1]], axis=0)
        joint = jnp.concatenate([window_in, previous], axis=-1).reshape(-1, 2 * C)
        act = jnp.dot(joint, w_cat, preferred_element_type=jnp.float32)
        filt = jnp.tanh(act[:, :C])
        gate = jax.nn.sigmoid(act[:, C:])
        hidden = (filt * gate).astype(jnp.bfloat16)
        tiled = hidden.reshape(TL, TILES, TILE, C)
        picked = tiled[:, neighbours].astype(jnp.float32)
        graph = jnp.einsum('jkpq,tjkqc->tjpc', adj_wide, picked).astype(jnp.bfloat16)
        both = jnp.concatenate([hidden, graph.reshape(-1, C)], axis=-1)
        cot_rows = window_cot.reshape(-1, C)
        mix_sum = mix_sum + jnp.dot(both.T, cot_rows, preferred_element_type=jnp.float32)
        back = jnp.dot(cot_rows, w_mixed.T, preferred_element_type=jnp.float32)
        direct = back[:, :C]
        graph_cot = back[:, C:].astype(jnp.bfloat16).reshape(TL, TILES, TILE, C)
        term = jnp.einsum('jkpq,tjpc->tjkqc', adj_wide, graph_cot.astype(jnp.float32)).astype(jnp.bfloat16)
        term_rows = jnp.transpose(term, (1, 2, 0, 3, 4)).reshape(TILES * NB, TL, TILE, C).astype(jnp.float32)
        summed = jax.ops.segment_sum(term_rows, flat_ids, num_segments=TILES)
        grad_hidden = direct + jnp.transpose(summed, (1, 0, 2, 3)).reshape(-1, C)
        act_cot = jnp.concatenate([grad_hidden * gate * (1.0 - filt * filt), grad_hidden * filt * gate * (1.0 - gate)], axis=-1).astype(jnp.bfloat16)
        conv_sum = conv_sum + jnp.dot(joint.T, act_cot, preferred_element_type=jnp.float32)
        back_in = jnp.dot(act_cot, w_cat.T, preferred_element_type=jnp.float32).reshape(TL, SITES, 2 * C)
        later = jnp.concatenate([back_in[1:, :, C:], jnp.zeros((1, SITES, C), jnp.float32)], axis=0)
        grad_in = (window_cot.astype(jnp.float32) + back_in[:, :, :C] + later).astype(jnp.bfloat16)
        return ((conv_sum, mix_sum), grad_in)
    start = (jnp.zeros((2 * C, 2 * C), jnp.float32), jnp.zeros((2 * C, C), jnp.float32))
    (conv_sum, mix_sum), grad_inputs = lax.scan(one_window, start, (inputs, cotangent))
    factor = 1.0 / math.sqrt(BATCH * TL * SITES)
    grad_filter = (conv_sum[:, :C] * factor).reshape(2, C, C)
    grad_gate = (conv_sum[:, C:] * factor).reshape(2, C, C)
    grad_mix = (mix_sum * factor).reshape(2, C, C)
    return (grad_inputs, grad_filter, grad_gate, grad_mix)
```

```python
import functools
import math

import jax
import jax.numpy as jnp
from jax import lax
from jax.experimental import pallas as pl
from jax.experimental.pallas import tpu as pltpu
from jax.sharding import PartitionSpec as P

MESH = pl.DeviceIdType.MESH
X = 4
TILE = 128
F32 = jnp.float32
BF16 = jnp.bfloat16


def dot(a, b, contract):
    return lax.dot_general(a, b, ((contract[:1], contract[1:]), ((), ())), preferred_element_type=F32)


class Reduction:
    def __init__(self, place, part, base, factor, scratch, sems, sends):
        self.place, self.part, self.base, self.factor, self.sends = place, part, base, factor, sends
        self.core, self.ysend, self.yrecv, self.xs, self.xrecv, self.zrecv, self.xg, self.yg, self.cg = scratch
        self.send, self.recv = sems
        self.count = self.core.shape[0]

    def copy(self, src, dst, sem, device):
        item = pltpu.make_async_remote_copy(
            src_ref=src, dst_ref=dst, send_sem=self.send.at[sem], recv_sem=self.recv.at[sem],
            device_id=device, device_id_type=MESH,
        )
        item.start()
        self.sends.append(item)
        return item

    def wait(self, items):
        for item in items:
            item.wait_recv()

    def start_core(self):
        p = self.place
        half = TILE
        other = pl.ds(pl.multiple_of((1 - p.c) * half, half), half)
        self.items = [self.copy(self.part.at[pl.ds(self.base, self.count), other], self.core, 0, p.sibling)]

    def start_y(self):
        p = self.place
        self.wait(self.items)
        rows = TILE // p.Y
        mine = pl.ds(pl.multiple_of(p.c * TILE, TILE), TILE)
        for i in range(self.count):
            total = self.core[i] + self.part[self.base + i, mine]
            self.core[i] = total
            self.ysend[:, i] = total.astype(BF16).reshape(p.Y, rows, total.shape[-1])
        self.items = [
            self.copy(self.ysend.at[lax.rem(p.y + i, p.Y)], self.yrecv.at[i - 1], i, p.along_y(i))
            for i in range(1, p.Y)
        ]

    def start_x(self):
        p = self.place
        self.wait(self.items)
        rows = TILE // p.Y
        half = rows // 2
        for i in range(self.count):
            total = self.core[i, pl.ds(pl.multiple_of(p.y * rows, rows), rows)]
            for j in range(p.Y - 1):
                total = total + self.yrecv[j, i].astype(F32)
            for q in range(X):
                top, left = (q // 2) * half, (q % 2) * 128
                self.xs[q, i] = total[top:top + half, left:left + 128]
        self.items = [
            self.copy(self.xs.at[lax.rem(p.x + i, X)], self.xrecv.at[i - 1], p.Y + i, p.along_x(i))
            for i in range(1, X)
        ]

    def start_z(self):
        p = self.place
        self.wait(self.items)
        total = self.xs[p.x]
        for j in range(X - 1):
            total = total + self.xrecv[j]
        self.zrecv[p.z] = total
        self.items = [
            self.copy(self.zrecv.at[p.z], self.zrecv.at[p.z], p.Y + X + i, p.along_z(i))
            for i in range(1, p.Z)
        ]

    def start_gather_x(self):
        p = self.place
        self.wait(self.items)
        total = self.zrecv[0]
        for j in range(1, p.Z):
            total = total + self.zrecv[j]
        self.xg[p.x] = total * self.factor
        self.items = [
            self.copy(self.xg.at[p.x], self.xg.at[p.x], p.Y + X + p.Z + i, p.along_x(i))
            for i in range(1, X)
        ]

    def start_gather_y(self):
        p = self.place
        self.wait(self.items)
        for i in range(self.count):
            rows = [jnp.concatenate([self.xg[2 * r, i], self.xg[2 * r + 1, i]], axis=1) for r in range(2)]
            self.yg[p.y, i] = jnp.concatenate(rows, axis=0).astype(BF16)
        self.items = [
            self.copy(self.yg.at[p.y], self.yg.at[p.y], p.Y + 2 * X + p.Z + i, p.along_y(i))
            for i in range(1, p.Y)
        ]

    def start_gather_core(self):
        p = self.place
        self.wait(self.items)
        self.items = [self.copy(self.yg, self.cg, 2 * p.Y + 2 * X + p.Z, p.sibling)]

    def finish(self, outs):
        p = self.place
        for source, core in ((self.yg, p.c), (self.cg, 1 - p.c)):
            if source is self.cg:
                self.wait(self.items)
            rows = pl.ds(pl.multiple_of(core * TILE, TILE), TILE)
            for i, (ref, tap) in enumerate(outs):
                block = source[:, i].reshape(TILE, ref.shape[-1])
                ref[tap, rows] = block.astype(F32)


class Place:
    def __init__(self, Y, Z):
        self.Y, self.Z = Y, Z
        self.dp = lax.axis_index("dp")
        self.region = lax.axis_index("region")
        self.x, self.y = lax.div(self.dp, Y), lax.rem(self.dp, Y)
        self.z, self.c = lax.div(self.region, 2), lax.rem(self.region, 2)
        self.sibling = (self.dp, self.z * 2 + 1 - self.c)

    def along_x(self, i):
        return (lax.rem(self.x + i, X) * self.Y + self.y, self.region)

    def along_y(self, i):
        return (self.x * self.Y + lax.rem(self.y + i, self.Y), self.region)

    def along_z(self, i):
        return (self.dp, lax.rem(self.z + i, self.Z) * 2 + self.c)


def kernel(Y, Z, factor, nbr, x_ref, cot_ref, wf, wg, wm, adj,
           gi_ref, gf_ref, gg_ref, gm_ref,
           gall, hall, asend, arecv, afull, bmat, fmat, acc, hacc, f1, f2, actcot, part, table, *rest):
    big, small = rest[:9], rest[9:18]
    ring_send, ring_recv, sib_send, sib_recv, adj_send, adj_recv, big_send, big_recv, small_send, small_recv = rest[18:]
    p = Place(Y, Z)
    R = 2 * Z
    per_tile = nbr.shape[1]
    entries = 2 * per_tile
    rows = TILE // Y
    sends = []

    barrier = pltpu.get_barrier_semaphore()
    partners = [(p.dp, lax.rem(p.region + i, R)) for i in range(1, R)]
    partners += [p.along_y(i) for i in range(1, Y)] + [p.along_x(i) for i in range(1, X)]
    for device in partners:
        pl.semaphore_signal(barrier, inc=1, device_id=device, device_id_type=MESH)

    def remote(src, dst, send, recv, device):
        item = pltpu.make_async_remote_copy(
            src_ref=src, dst_ref=dst, send_sem=send, recv_sem=recv, device_id=device, device_id_type=MESH)
        item.start()
        sends.append(item)

    def arrived(ref, send, recv):
        pltpu.make_async_remote_copy(
            src_ref=ref, dst_ref=ref, send_sem=send, recv_sem=recv, device_id=p.sibling, device_id_type=MESH
        ).wait_recv()

    def origin(direction, step):
        return lax.rem(p.z + (Z - step if direction == 0 else step), Z)

    def ring(stream, buf, step):
        for tile in range(2):
            for direction in range(2):
                slot = origin(direction, step) * 2 + p.c
                block = buf.at[direction, slot, tile]
                if step > 0:
                    arrived(block, ring_send.at[stream, direction, step - 1, tile],
                            ring_recv.at[stream, direction, step - 1, tile])
                if step < Z - 1:
                    remote(block, block, ring_send.at[stream, direction, step, tile],
                           ring_recv.at[stream, direction, step, tile], p.along_z(1 if direction == 0 else Z - 1))
                remote(block, block, sib_send.at[stream, direction, step, tile],
                       sib_recv.at[stream, direction, step, tile], p.sibling)

    def from_sibling(stream, buf, step):
        for tile in range(2):
            for direction in range(2):
                slot = origin(direction, step) * 2 + 1 - p.c
                arrived(buf.at[direction, slot, tile], sib_send.at[stream, direction, step, tile],
                        sib_recv.at[stream, direction, step, tile])

    def pair(buf, t, chip, choice):
        halves = []
        for core in range(2):
            region = chip * 2 + core
            first = table[choice, region] == 0
            halves.append(jnp.where(first, buf[t, region, 0], buf[t, region, 1]))
        return jnp.concatenate(halves, axis=0)

    for t in range(2):
        gall[t, p.region] = dot(cot_ref[t], wm[1], (1, 1)).astype(BF16).reshape(2, TILE, -1)
    pl.semaphore_wait(barrier, len(partners))
    ring(0, gall, 0)

    def scan(region, carry):
        entry = valid = own = named = other = mine = jnp.int32(0)
        for e in range(entries):
            a = nbr[p.region * 2 + e // per_tile, e % per_tile]
            hit = lax.div(a, 2) == region
            entry = jnp.where(hit, e, entry)
            valid = jnp.where(hit, 1, valid)
            own = jnp.where(hit, e // per_tile, own)
            named = jnp.where(hit, lax.rem(a, 2), named)
            b = nbr[region * 2 + e // per_tile, e % per_tile]
            back = lax.div(b, 2) == p.region
            other = jnp.where(back, e // per_tile, other)
            mine = jnp.where(back, lax.rem(b, 2), mine)
        for row, value in enumerate((entry, valid, own, named, other, mine)):
            table[row, region] = value
        return carry
    lax.fori_loop(0, R, scan, 0)

    def fill(region, carry):
        block = adj[table[0, region], pl.ds(pl.multiple_of(p.y * rows, rows), rows)]
        asend[region] = jnp.where(table[1, region] == 1, block, jnp.zeros_like(block))
        return carry
    lax.fori_loop(0, R, fill, 0)
    arecv[p.region] = asend[p.region]
    for i in range(1, R):
        target = lax.rem(p.region + i, R)
        remote(asend.at[target], arecv.at[p.region], adj_send.at[i], adj_recv.at[i], (p.dp, target))

    for t in range(2):
        pre_f = dot(x_ref[t], wf[0], (1, 0))
        pre_g = dot(x_ref[t], wg[0], (1, 0))
        if t == 1:
            pre_f = pre_f + dot(x_ref[0], wf[1], (1, 0))
            pre_g = pre_g + dot(x_ref[0], wg[1], (1, 0))
        filt = jnp.tanh(pre_f)
        gate = jax.nn.sigmoid(pre_g)
        both = filt * gate
        hall[t, p.region] = both.astype(BF16).reshape(2, TILE, -1)
        f1[t] = gate * (1.0 - filt * filt)
        f2[t] = both * (1.0 - gate)
    ring(0, gall, 1)

    for i in range(1, R):
        source = lax.rem(p.region + R - i, R)
        arrived(arecv.at[source], adj_send.at[i], adj_recv.at[i])
    afull[p.y] = arecv[...]
    for i in range(1, Y):
        remote(arecv, afull.at[p.y], adj_send.at[R + i], adj_recv.at[R + i], p.along_y(i))
    for t in range(2):
        acc[t] = dot(cot_ref[t], wm[0], (1, 1))
        own = hall[t, p.region].reshape(2 * TILE, -1)
        here = dot(own, cot_ref[t], (0, 0))
        part[4] = here if t == 0 else part[4] + here
    ring(0, gall, 2)

    def build_forward(chip, carry):
        for core in range(2):
            region = chip * 2 + core
            block = adj[table[0, region]]
            zero = jnp.zeros_like(block)
            own = jnp.where(table[1, region] == 1, table[2, region], 2)
            for j in range(2):
                fmat[chip, j * TILE:(j + 1) * TILE, core * TILE:(core + 1) * TILE] = jnp.where(own == j, block, zero)
        return carry
    lax.fori_loop(0, Z, build_forward, 0)
    for i in range(1, Y):
        source = lax.rem(p.y + Y - i, Y)
        arrived(afull.at[source], adj_send.at[R + i], adj_recv.at[R + i])

    def build_backward(chip, carry):
        for core in range(2):
            region = chip * 2 + core
            block = afull[:, region].reshape(TILE, TILE)
            zero = jnp.zeros_like(block)
            for j in range(2):
                bmat[chip, core * TILE:(core + 1) * TILE, j * TILE:(j + 1) * TILE] = jnp.where(
                    table[5, region] == j, block, zero)
        return carry
    lax.fori_loop(0, Z, build_backward, 0)

    def backward(step):
        from_sibling(0, gall, step)
        for t in range(2):
            chip = origin(t, step)
            acc[t] += dot(bmat[chip], pair(gall, t, chip, 4), (0, 0))

    def forward(step):
        from_sibling(1, hall, step)
        for t in range(2):
            chip = origin(t, step)
            more = dot(fmat[chip], pair(hall, t, chip, 3), (1, 0))
            hacc[t] = more if step == 0 else hacc[t] + more

    backward(0)
    done = 1
    for step in range(3, Z):
        ring(0, gall, step)
        while done < step:
            backward(done)
            done += 1
    ring(1, hall, 0)
    while done < Z:
        backward(done)
        done += 1

    one = Reduction(p, part, 0, factor, big, (big_send, big_recv), sends)
    two = Reduction(p, part, 5, factor, small, (small_send, small_recv), sends)

    for t in range(2):
        actcot[t, :, :256] = (acc[t] * f1[t]).astype(BF16)
        actcot[t, :, 256:] = (acc[t] * f2[t]).astype(BF16)
    ring(1, hall, 1)
    second = dot(x_ref[0], actcot[1], (0, 0))
    part[1] = second[:, :256]
    part[3] = second[:, 256:]
    first = dot(x_ref[0], actcot[0], (0, 0)) + dot(x_ref[1], actcot[1], (0, 0))
    part[0] = first[:, :256]
    part[2] = first[:, 256:]
    one.start_core()
    forward(0)
    if Z > 2:
        ring(1, hall, 2)
    for t in range(2):
        total = cot_ref[t].astype(F32)
        for tap in range(2 - t):
            a = actcot[t + tap]
            total = total + dot(a[:, :256], wf[tap], (1, 1)) + dot(a[:, 256:], wg[tap], (1, 1))
        gi_ref[t] = total.astype(BF16)
    one.start_y()
    done = 1
    stages = {5: one.start_x, 6: one.start_z}
    for step in range(3, Z):
        ring(1, hall, step)
        while done < step:
            forward(done)
            done += 1
        if step in stages:
            stages.pop(step)()
    while done < Z:
        forward(done)
        done += 1
    for t in range(2):
        here = dot(hacc[t].astype(BF16), cot_ref[t], (0, 0))
        part[5] = here if t == 0 else part[5] + here
    two.start_core()
    for stage in stages.values():
        stage()
    one.start_gather_x()
    two.start_y()
    one.start_gather_y()
    two.start_x()
    two.start_z()
    two.start_gather_x()
    one.start_gather_core()
    two.start_gather_y()
    two.start_gather_core()
    one.finish([(gf_ref, 0), (gf_ref, 1), (gg_ref, 0), (gg_ref, 1), (gm_ref, 0)])
    two.finish([(gm_ref, 1)])
    for item in sends:
        item.wait_send()


def reduction_scratch(count, chans, Y, Z):
    rows = TILE // Y
    return [
        pltpu.VMEM((count, TILE, chans), F32),
        pltpu.VMEM((Y, count, rows, chans), BF16),
        pltpu.VMEM((Y - 1, count, rows, chans), BF16),
        pltpu.VMEM((X, count, rows // 2, 128), F32),
        pltpu.VMEM((X - 1, count, rows // 2, 128), F32),
        pltpu.VMEM((Z, count, rows // 2, 128), F32),
        pltpu.VMEM((X, count, rows // 2, 128), F32),
        pltpu.VMEM((Y, count, rows, chans), BF16),
        pltpu.VMEM((Y, count, rows, chans), BF16),
    ]


def solution(mesh):
    Y, Z = mesh.shape["dp"] // X, mesh.shape["region"] // 2
    R = 2 * Z

    def per_device(inputs, cotangent, w_filter, w_gate, w_mix, neighbours, adjacency):
        _, steps, sites, chans = inputs.shape
        total_rows = steps * sites * mesh.shape["dp"] * R
        per_tile = neighbours.shape[1]
        dma = pltpu.SemaphoreType.DMA
        stages = 2 * Y + 2 * X + Z + 1
        vmem = pl.BlockSpec(memory_space=pltpu.VMEM)
        grads = jax.ShapeDtypeStruct((2, chans, chans), F32)
        grad_inputs, grad_filter, grad_gate, grad_mix = pl.pallas_call(
            functools.partial(kernel, Y, Z, 1.0 / math.sqrt(total_rows)),
            out_shape=(jax.ShapeDtypeStruct((steps, sites, chans), BF16), grads, grads, grads),
            in_specs=[pl.BlockSpec(memory_space=pltpu.SMEM)] + [vmem] * 6,
            out_specs=(vmem,) * 4,
            scratch_shapes=[
                pltpu.VMEM((2, R, 2, TILE, chans), BF16),
                pltpu.VMEM((2, R, 2, TILE, chans), BF16),
                pltpu.VMEM((R, TILE // Y, TILE), BF16),
                pltpu.VMEM((R, TILE // Y, TILE), BF16),
                pltpu.VMEM((Y, R, TILE // Y, TILE), BF16),
                pltpu.VMEM((Z, 2 * TILE, 2 * TILE), BF16),
                pltpu.VMEM((Z, 2 * TILE, 2 * TILE), BF16),
                pltpu.VMEM((2, sites, chans), F32),
                pltpu.VMEM((2, sites, chans), F32),
                pltpu.VMEM((2, sites, chans), F32),
                pltpu.VMEM((2, sites, chans), F32),
                pltpu.VMEM((2, sites, 2 * chans), BF16),
                pltpu.VMEM((6, chans, chans), F32),
                pltpu.SMEM((6, R), jnp.int32),
                *reduction_scratch(5, chans, Y, Z),
                *reduction_scratch(1, chans, Y, Z),
                dma((2, 2, Z, 2)), dma((2, 2, Z, 2)),
                dma((2, 2, Z, 2)), dma((2, 2, Z, 2)),
                dma((R + Y,)), dma((R + Y,)),
                dma((stages,)), dma((stages,)),
                dma((stages,)), dma((stages,)),
            ],
            compiler_params=pltpu.CompilerParams(
                collective_id=0, has_side_effects=True, vmem_limit_bytes=48 << 20),
            name="train_step",
        )(neighbours, inputs[0], cotangent[0], w_filter, w_gate, w_mix,
          adjacency.reshape(2 * per_tile, TILE, TILE))
        return grad_inputs[None], grad_filter, grad_gate, grad_mix

    return jax.shard_map(
        per_device,
        mesh=mesh,
        in_specs=(
            P("dp", None, "region", None),
            P("dp", None, "region", None),
            P(),
            P(),
            P(),
            P(),
            P("region", None, None, None),
        ),
        out_specs=(P("dp", None, "region", None), P(), P(), P()),
        check_vma=False,
    )
```

```python
import functools
import math

import jax
import jax.numpy as jnp
from jax import lax
from jax.experimental import pallas as pl
from jax.experimental.pallas import tpu as pltpu
from jax.sharding import PartitionSpec as P

MESH = pl.DeviceIdType.MESH
X = 4
TILE = 128
CHUNKS = 4
ORDERS = ("yxz", "zyx", "xzy")
F32 = jnp.float32
BF16 = jnp.bfloat16


def dot(a, b, contract):
    return lax.dot_general(a, b, ((contract[:1], contract[1:]), ((), ())), preferred_element_type=F32)


class Place:
    def __init__(self, Y, Z):
        self.size = {"x": X, "y": Y, "z": Z}
        self.dp = lax.axis_index("dp")
        self.region = lax.axis_index("region")
        self.at = {
            "x": lax.div(self.dp, Y), "y": lax.rem(self.dp, Y), "z": lax.div(self.region, 2),
        }
        self.c = lax.rem(self.region, 2)
        self.sibling = (self.dp, self.at["z"] * 2 + 1 - self.c)

    def along(self, axis, i):
        at = dict(self.at)
        at[axis] = lax.rem(at[axis] + i, self.size[axis])
        return (at["x"] * self.size["y"] + at["y"], at["z"] * 2 + self.c)


class Reduction:
    def __init__(self, place, order, part, base, factor, scratch, sems, sends):
        self.p, self.order, self.part, self.base, self.factor, self.sends = place, order, part, base, factor, sends
        self.core, self.s1, self.r1, self.s2, self.r2, self.x3, self.g2, self.g1, self.cg = scratch
        self.send, self.recv = sems
        self.items, self.used = [], 0

    def copy(self, src, dst, device):
        item = pltpu.make_async_remote_copy(
            src_ref=src, dst_ref=dst, send_sem=self.send.at[self.used], recv_sem=self.recv.at[self.used],
            device_id=device, device_id_type=MESH,
        )
        self.used += 1
        item.start()
        self.sends.append(item)
        self.items.append(item)

    def wait(self):
        for item in self.items:
            item.wait_recv()
        self.items = []

    def peers(self, k):
        axis = self.order[k]
        n, at = self.p.size[axis], self.p.at[axis]
        return n, at, [(i, lax.rem(at + i, n), self.p.along(axis, i)) for i in range(1, n)]

    def start_core(self):
        other = pl.ds(pl.multiple_of((1 - self.p.c) * TILE, TILE), TILE)
        self.copy(self.part.at[pl.ds(self.base, 2), other], self.core, self.p.sibling)

    def start_first(self):
        self.wait()
        n, at, peers = self.peers(0)
        mine = pl.ds(pl.multiple_of(self.p.c * TILE, TILE), TILE)
        for i in range(2):
            total = self.core[i] + self.part[self.base + i, mine]
            self.core[i] = total
            self.s1[:, i] = total.astype(BF16).reshape(n, TILE // n, total.shape[-1])
        for i, slot, device in peers:
            self.copy(self.s1.at[slot], self.r1.at[i - 1], device)

    def start_second(self):
        self.wait()
        first, at, _ = self.peers(0)
        rows = TILE // first
        tiles = []
        for i in range(2):
            total = self.core[i, pl.ds(pl.multiple_of(at * rows, rows), rows)]
            for j in range(first - 1):
                total = total + self.r1[j, i].astype(F32)
            tiles += [
                total[r * 8:r * 8 + 8, h * 128:h * 128 + 128] for r in range(rows // 8) for h in range(2)
            ]
        n, at, peers = self.peers(1)
        each = len(tiles) // n
        for index, tile in enumerate(tiles):
            self.s2[index // each, index % each] = tile
        for i, slot, device in peers:
            self.copy(self.s2.at[slot], self.r2.at[i - 1], device)

    def start_third(self):
        self.wait()
        n, at, _ = self.peers(1)
        total = self.s2[at]
        for j in range(n - 1):
            total = total + self.r2[j]
        n, at, peers = self.peers(2)
        self.x3[at] = total
        for i, slot, device in peers:
            self.copy(self.x3.at[at], self.x3.at[at], device)

    def start_gather_second(self):
        self.wait()
        total = self.x3[0]
        for j in range(1, self.peers(2)[0]):
            total = total + self.x3[j]
        n, at, peers = self.peers(1)
        self.g2[at] = total * self.factor
        for i, slot, device in peers:
            self.copy(self.g2.at[at], self.g2.at[at], device)

    def start_gather_first(self):
        self.wait()
        n, at, peers = self.peers(0)
        each = self.g2.shape[1]
        tiles = [self.g2[i, j] for i in range(self.g2.shape[0]) for j in range(each)]
        for i in range(2):
            mine = tiles[i * len(tiles) // 2:(i + 1) * len(tiles) // 2]
            rows = [jnp.concatenate(mine[r:r + 2], axis=1) for r in range(0, len(mine), 2)]
            self.g1[at, i] = jnp.concatenate(rows, axis=0).astype(BF16)
        for i, slot, device in peers:
            self.copy(self.g1.at[at], self.g1.at[at], device)

    def start_gather_core(self):
        self.wait()
        self.copy(self.g1, self.cg, self.p.sibling)

    def finish(self, out):
        for source, core in ((self.g1, self.p.c), (self.cg, 1 - self.p.c)):
            if source is self.cg:
                self.wait()
            rows = pl.ds(pl.multiple_of(core * TILE, TILE), TILE)
            for i in range(2):
                out[self.base + i, rows] = source[:, i].reshape(TILE, out.shape[-1]).astype(F32)


def kernel(Y, Z, factor, nbr, x_hbm, cot_hbm, wf_hbm, wg_hbm, wm_hbm, adj_hbm,
           gi_ref, out_ref,
           x_ref, wf, wg, wm, adj, gall, asend, arecv, afull, bmat, direct, acc, hid, f1, f2, actcot, part, table,
           *rest):
    scratch = [rest[9 * i:9 * i + 9] for i in range(3)]
    local_sem, ring_send, ring_recv, sib_send, sib_recv, adj_send, adj_recv = rest[27:34]
    sems = [rest[34 + 2 * i:36 + 2 * i] for i in range(3)]
    p = Place(Y, Z)
    R = 2 * Z
    per_tile = nbr.shape[0]
    entries = 2 * per_tile
    rows = TILE // Y
    sends = []

    def fetch(i, src, dst):
        item = pltpu.make_async_copy(src, dst, local_sem.at[i])
        item.start()
        return item

    get_cot = [fetch(t, cot_hbm.at[t], gall.at[t, p.region]) for t in range(2)]
    get_adj = fetch(2, adj_hbm, adj)
    get_x = fetch(3, x_hbm, x_ref)
    get_wf = fetch(4, wf_hbm, wf)
    get_wg = fetch(5, wg_hbm, wg)
    get_wm = fetch(6, wm_hbm, wm)

    barrier = pltpu.get_barrier_semaphore()
    partners = [(p.dp, lax.rem(p.region + i, R)) for i in range(1, R)]
    partners += [p.along(axis, i) for axis, n in (("x", X), ("y", Y)) for i in range(1, n)]
    for device in partners:
        pl.semaphore_signal(barrier, inc=1, device_id=device, device_id_type=MESH)

    def remote(src, dst, send, recv, device):
        item = pltpu.make_async_remote_copy(
            src_ref=src, dst_ref=dst, send_sem=send, recv_sem=recv, device_id=device, device_id_type=MESH)
        item.start()
        sends.append(item)

    def arrived(ref, send, recv):
        pltpu.make_async_remote_copy(
            src_ref=ref, dst_ref=ref, send_sem=send, recv_sem=recv, device_id=p.sibling, device_id_type=MESH
        ).wait_recv()

    def origin(direction, step):
        return lax.rem(p.at["z"] + (Z - step if direction == 0 else step), Z)

    piece = 2 * TILE // CHUNKS

    def ring(step):
        for chunk in range(CHUNKS):
            for direction in range(2):
                block = gall.at[direction, origin(direction, step) * 2 + p.c, pl.ds(chunk * piece, piece)]
                if step > 0:
                    arrived(block, ring_send.at[direction, step - 1, chunk], ring_recv.at[direction, step - 1, chunk])
                if step < Z - 1:
                    remote(block, block, ring_send.at[direction, step, chunk], ring_recv.at[direction, step, chunk],
                           p.along("z", 1 if direction == 0 else Z - 1))
        for direction in range(2):
            block = gall.at[direction, origin(direction, step) * 2 + p.c]
            remote(block, block, sib_send.at[direction, step], sib_recv.at[direction, step], p.sibling)

    def scan(region, carry):
        entry = valid = other = mine = jnp.int32(0)
        for e in range(entries):
            a = nbr[e % per_tile, p.region * 2 + e // per_tile]
            hit = lax.div(a, 2) == region
            entry = jnp.where(hit, e, entry)
            valid = jnp.where(hit, 1, valid)
            b = nbr[e % per_tile, region * 2 + e // per_tile]
            back = lax.div(b, 2) == p.region
            other = jnp.where(back, e // per_tile, other)
            mine = jnp.where(back, lax.rem(b, 2), mine)
        for row, value in enumerate((entry, valid, other, mine)):
            table[row, region] = value
        return carry

    def fill(region, carry):
        block = adj[table[0, region], pl.ds(pl.multiple_of(p.at["y"] * rows, rows), rows)]
        asend[region] = jnp.where(table[1, region] == 1, block, jnp.zeros_like(block))
        return carry

    def forward(t):
        pre_f = dot(x_ref[t], wf[0], (1, 0))
        pre_g = dot(x_ref[t], wg[0], (1, 0))
        if t == 1:
            pre_f = pre_f + dot(x_ref[0], wf[1], (1, 0))
            pre_g = pre_g + dot(x_ref[0], wg[1], (1, 0))
        filt = jnp.tanh(pre_f)
        gate = jax.nn.sigmoid(pre_g)
        both = filt * gate
        hid[t] = both.astype(BF16)
        f1[t] = gate * (1.0 - filt * filt)
        f2[t] = both * (1.0 - gate)

    def own_products():
        for t in range(2):
            cot = gall[t, p.region]
            direct[t] = dot(cot, wm[0], (1, 1))
            here = dot(hid[t], cot, (0, 0))
            part[0] = here if t == 0 else part[0] + here

    def send_adjacency():
        arecv[p.region] = asend[p.region]
        for i in range(1, R):
            target = lax.rem(p.region + i, R)
            remote(asend.at[target], arecv.at[p.region], adj_send.at[i], adj_recv.at[i], (p.dp, target))

    def share_adjacency():
        for i in range(1, R):
            source = lax.rem(p.region + R - i, R)
            arrived(arecv.at[source], adj_send.at[i], adj_recv.at[i])
        for i in range(1, Y):
            remote(arecv, afull.at[p.at["y"]], adj_send.at[R + i], adj_recv.at[R + i], p.along("y", i))
        afull[p.at["y"]] = arecv[...]

    def wait_adjacency():
        for i in range(1, Y):
            source = lax.rem(p.at["y"] + Y - i, Y)
            arrived(afull.at[source], adj_send.at[R + i], adj_recv.at[R + i])

    def build(chip, carry):
        for core in range(2):
            region = chip * 2 + core
            block = afull[:, region].reshape(TILE, TILE).T
            zero = jnp.zeros_like(block)
            for j in range(2):
                bmat[chip, j * TILE:(j + 1) * TILE, core * TILE:(core + 1) * TILE] = jnp.where(
                    table[3, region] == j, block, zero)
        return carry

    def gathered(step):
        for direction in range(2):
            block = gall.at[direction, origin(direction, step) * 2 + 1 - p.c]
            arrived(block, sib_send.at[direction, step], sib_recv.at[direction, step])
        for t in range(2):
            chip = origin(t, step)
            halves = []
            for core in range(2):
                region = chip * 2 + core
                halves.append(jnp.where(table[2, region] == 0, gall[t, region, :TILE], gall[t, region, TILE:]))
            more = dot(bmat[chip], jnp.concatenate(halves, axis=0), (1, 0))
            acc[t] = more if step == 0 else acc[t] + more

    for item in get_cot:
        item.wait()
    pl.semaphore_wait(barrier, len(partners))
    ring(0)
    lax.fori_loop(0, R, scan, 0)
    get_adj.wait()
    lax.fori_loop(0, R, fill, 0)
    send_adjacency()
    ring(1)
    for item in (get_x, get_wf, get_wg):
        item.wait()
    forward(0)
    ring(2)
    share_adjacency()
    forward(1)
    get_wm.wait()
    ring(3)
    own_products()
    work = [wait_adjacency, lambda: lax.fori_loop(0, Z, build, 0)]
    work += [functools.partial(gathered, step) for step in range(Z - 1)]
    per_step = -(-len(work) // max(1, Z - 4))
    for step in range(4, Z):
        ring(step)
        for item in work[:per_step]:
            item()
        work = work[per_step:]
    for item in work:
        item()
    gathered(Z - 1)

    groups = [
        Reduction(p, order, part, 2 * i, factor, scratch[i], sems[i], sends) for i, order in enumerate(ORDERS)
    ]
    mixed = [acc[t].astype(BF16) for t in range(2)]
    part[1] = dot(hid[0], mixed[0], (0, 0)) + dot(hid[1], mixed[1], (0, 0))
    groups[0].start_core()
    for t in range(2):
        grad = direct[t] + dot(mixed[t], wm[1], (1, 1))
        actcot[0, t] = (grad * f1[t]).astype(BF16)
        actcot[1, t] = (grad * f2[t]).astype(BF16)
    for g in range(2):
        part[2 + 2 * g] = dot(x_ref[0], actcot[g, 0], (0, 0)) + dot(x_ref[1], actcot[g, 1], (0, 0))
        part[3 + 2 * g] = dot(x_ref[0], actcot[g, 1], (0, 0))
        groups[1 + g].start_core()
    for group in groups:
        group.start_first()
    for t in range(2):
        total = gall[t, p.region].astype(F32)
        for tap in range(2 - t):
            total = total + dot(actcot[0, t + tap], wf[tap], (1, 1)) + dot(actcot[1, t + tap], wg[tap], (1, 1))
        gi_ref[t] = total.astype(BF16)
    for stage in ("start_second", "start_third", "start_gather_second", "start_gather_first", "start_gather_core"):
        for group in groups:
            getattr(group, stage)()
    for group in groups:
        group.finish(out_ref)
    for item in sends:
        item.wait_send()


def write(gi, grads, gi_out, gf_out, gg_out, gm_out, sem):
    copies = [
        pltpu.make_async_copy(gi, gi_out, sem.at[0]),
        pltpu.make_async_copy(grads.at[pl.ds(0, 2)], gm_out, sem.at[1]),
        pltpu.make_async_copy(grads.at[pl.ds(2, 2)], gf_out, sem.at[2]),
        pltpu.make_async_copy(grads.at[pl.ds(4, 2)], gg_out, sem.at[3]),
    ]
    for item in copies:
        item.start()
    for item in copies:
        item.wait()


def reduction_scratch(order, chans, sizes):
    n1, n2, n3 = (sizes[axis] for axis in order)
    each = 2 * (TILE // n1 // 8) * (chans // 128) // n2
    return [
        pltpu.VMEM((2, TILE, chans), F32),
        pltpu.VMEM((n1, 2, TILE // n1, chans), BF16),
        pltpu.VMEM((n1 - 1, 2, TILE // n1, chans), BF16),
        pltpu.VMEM((n2, each, 8, 128), F32),
        pltpu.VMEM((n2 - 1, each, 8, 128), F32),
        pltpu.VMEM((n3, each, 8, 128), F32),
        pltpu.VMEM((n2, each, 8, 128), F32),
        pltpu.VMEM((n1, 2, TILE // n1, chans), BF16),
        pltpu.VMEM((n1, 2, TILE // n1, chans), BF16),
    ]


def solution(mesh):
    Y, Z = mesh.shape["dp"] // X, mesh.shape["region"] // 2
    R = 2 * Z
    sizes = {"x": X, "y": Y, "z": Z}

    def per_device(inputs, cotangent, w_filter, w_gate, w_mix, neighbours, adjacency):
        _, steps, sites, chans = inputs.shape
        total_rows = steps * sites * mesh.shape["dp"] * R
        per_tile = neighbours.shape[1]
        dma = pltpu.SemaphoreType.DMA
        vmem = pl.BlockSpec(memory_space=pltpu.VMEM)
        hbm = pl.BlockSpec(memory_space=pltpu.HBM)
        scratch, sems = [], []
        for order in ORDERS:
            scratch += reduction_scratch(order, chans, sizes)
            n1, n2, n3 = (sizes[axis] for axis in order)
            count = 2 + 2 * (n1 - 1) + 2 * (n2 - 1) + n3 - 1
            sems += [dma((count,)), dma((count,))]
        weights = pltpu.VMEM((2, chans, chans), BF16)
        wide = pltpu.VMEM((steps, sites, chans), F32)
        narrow = pltpu.VMEM((steps, sites, chans), BF16)
        grad_inputs, grads = pl.pallas_call(
            functools.partial(kernel, Y, Z, 1.0 / math.sqrt(total_rows)),
            out_shape=(
                jax.ShapeDtypeStruct((steps, sites, chans), BF16), jax.ShapeDtypeStruct((6, chans, chans), F32),
            ),
            in_specs=[pl.BlockSpec(memory_space=pltpu.SMEM)] + [hbm] * 6,
            out_specs=(vmem, vmem),
            scratch_shapes=[
                narrow, weights, weights, weights,
                pltpu.VMEM((2 * per_tile, TILE, TILE), BF16),
                pltpu.VMEM((steps, R, sites, chans), BF16),
                pltpu.VMEM((R, TILE // Y, TILE), BF16),
                pltpu.VMEM((R, TILE // Y, TILE), BF16),
                pltpu.VMEM((Y, R, TILE // Y, TILE), BF16),
                pltpu.VMEM((Z, 2 * TILE, 2 * TILE), BF16),
                wide, wide, narrow, wide, wide,
                pltpu.VMEM((2, steps, sites, chans), BF16),
                pltpu.VMEM((6, chans, chans), F32),
                pltpu.SMEM((4, R), jnp.int32),
                *scratch,
                dma((7,)),
                dma((2, Z, CHUNKS)), dma((2, Z, CHUNKS)),
                dma((2, Z)), dma((2, Z)),
                dma((R + Y,)), dma((R + Y,)),
                *sems,
            ],
            compiler_params=pltpu.CompilerParams(
                collective_id=0, has_side_effects=True, vmem_limit_bytes=56 << 20),
            name="train_step",
        )(neighbours.T, inputs[0], cotangent[0], w_filter, w_gate, w_mix,
          adjacency.reshape(2 * per_tile, TILE, TILE))
        grad = jax.ShapeDtypeStruct((2, chans, chans), F32)
        grad_inputs, grad_filter, grad_gate, grad_mix = pl.pallas_call(
            write,
            out_shape=(jax.ShapeDtypeStruct((steps, sites, chans), BF16), grad, grad, grad),
            in_specs=[pl.BlockSpec(memory_space=pl.ANY)] * 2,
            out_specs=(hbm,) * 4,
            scratch_shapes=[dma((4,))],
            name="write",
        )(grad_inputs, grads)
        return grad_inputs[None], grad_filter, grad_gate, grad_mix

    return jax.shard_map(
        per_device,
        mesh=mesh,
        in_specs=(
            P("dp", None, "region", None),
            P("dp", None, "region", None),
            P(),
            P(),
            P(),
            P(),
            P("region", None, None, None),
        ),
        out_specs=(P("dp", None, "region", None), P(), P(), P()),
        check_vma=False,
    )
```

```python
import functools
import math

import jax
import jax.numpy as jnp
from jax import lax
from jax.experimental import pallas as pl
from jax.experimental.pallas import tpu as pltpu
from jax.sharding import PartitionSpec as P

MESH = pl.DeviceIdType.MESH
X = 4
TILE = 128
ORDERS = ("yxz", "zxy", "xzy")
F32 = jnp.float32
BF16 = jnp.bfloat16


def dot(a, b, contract):
    return lax.dot_general(a, b, ((contract[:1], contract[1:]), ((), ())), preferred_element_type=F32)


class Place:
    def __init__(self, Y, Z):
        self.size = {"x": X, "y": Y, "z": Z}
        self.dp = lax.axis_index("dp")
        self.region = lax.axis_index("region")
        self.at = {
            "x": lax.div(self.dp, Y), "y": lax.rem(self.dp, Y), "z": lax.div(self.region, 2),
        }
        self.c = lax.rem(self.region, 2)
        self.sibling = (self.dp, self.at["z"] * 2 + 1 - self.c)

    def along(self, axis, i):
        at = dict(self.at)
        at[axis] = lax.rem(at[axis] + i, self.size[axis])
        return (at["x"] * self.size["y"] + at["y"], at["z"] * 2 + self.c)


class Reduction:
    def __init__(self, place, order, part, base, factor, scratch, sems, sends):
        self.p, self.order, self.part, self.base, self.factor, self.sends = place, order, part, base, factor, sends
        self.core, self.s1, self.r1, self.s2, self.r2, self.x3, self.g2, self.g1, self.cg = scratch
        self.send, self.recv = sems
        self.items, self.used = [], 0

    def copy(self, src, dst, device):
        item = pltpu.make_async_remote_copy(
            src_ref=src, dst_ref=dst, send_sem=self.send.at[self.used], recv_sem=self.recv.at[self.used],
            device_id=device, device_id_type=MESH,
        )
        self.used += 1
        item.start()
        self.sends.append(item)
        self.items.append(item)

    def wait(self):
        for item in self.items:
            item.wait_recv()
        self.items = []

    def peers(self, k):
        axis = self.order[k]
        n, at = self.p.size[axis], self.p.at[axis]
        return n, at, [(i, lax.rem(at + i, n), self.p.along(axis, i)) for i in range(1, n)]

    def start_core(self):
        other = pl.ds(pl.multiple_of((1 - self.p.c) * TILE, TILE), TILE)
        self.copy(self.part.at[pl.ds(self.base, 2), other], self.core, self.p.sibling)

    def start_first(self):
        self.wait()
        n, at, peers = self.peers(0)
        mine = pl.ds(pl.multiple_of(self.p.c * TILE, TILE), TILE)
        for i in range(2):
            total = self.core[i] + self.part[self.base + i, mine]
            self.core[i] = total
            self.s1[:, i] = total.astype(BF16).reshape(n, TILE // n, total.shape[-1])
        for i, slot, device in peers:
            self.copy(self.s1.at[slot], self.r1.at[i - 1], device)

    def start_second(self):
        self.wait()
        first, at, _ = self.peers(0)
        rows = TILE // first
        tiles = []
        for i in range(2):
            total = self.core[i, pl.ds(pl.multiple_of(at * rows, rows), rows)]
            for j in range(first - 1):
                total = total + self.r1[j, i].astype(F32)
            tiles += [
                total[r * 8:r * 8 + 8, h * 128:h * 128 + 128] for r in range(rows // 8) for h in range(2)
            ]
        n, at, peers = self.peers(1)
        each = len(tiles) // n
        for index, tile in enumerate(tiles):
            self.s2[index // each, index % each] = tile
        for i, slot, device in peers:
            self.copy(self.s2.at[slot], self.r2.at[i - 1], device)

    def start_third(self):
        self.wait()
        n, at, _ = self.peers(1)
        total = self.s2[at]
        for j in range(n - 1):
            total = total + self.r2[j]
        n, at, peers = self.peers(2)
        self.x3[at] = total
        for i, slot, device in peers:
            self.copy(self.x3.at[at], self.x3.at[at], device)

    def start_gather_second(self):
        self.wait()
        total = self.x3[0]
        for j in range(1, self.peers(2)[0]):
            total = total + self.x3[j]
        n, at, peers = self.peers(1)
        self.g2[at] = total * self.factor
        for i, slot, device in peers:
            self.copy(self.g2.at[at], self.g2.at[at], device)

    def start_gather_first(self):
        self.wait()
        n, at, peers = self.peers(0)
        each = self.g2.shape[1]
        tiles = [self.g2[i, j] for i in range(self.g2.shape[0]) for j in range(each)]
        for i in range(2):
            mine = tiles[i * len(tiles) // 2:(i + 1) * len(tiles) // 2]
            rows = [jnp.concatenate(mine[r:r + 2], axis=1) for r in range(0, len(mine), 2)]
            self.g1[at, i] = jnp.concatenate(rows, axis=0).astype(BF16)
        for i, slot, device in peers:
            self.copy(self.g1.at[at], self.g1.at[at], device)

    def start_gather_core(self):
        self.wait()
        self.copy(self.g1, self.cg, self.p.sibling)

    def put(self, out, sem, other):
        source, core = (self.cg, 1 - self.p.c) if other else (self.g1, self.p.c)
        copies = [
            pltpu.make_async_copy(source.at[:, i], out.at[i, core], sem.at[other, self.base + i]) for i in range(2)
        ]
        for item in copies:
            item.start()
        return copies


def kernel(Y, Z, factor, nbr, x_hbm, cot_hbm, wf_hbm, wg_hbm, wm_hbm, adj_hbm,
           gi_ref, out_mix, out_filter, out_gate,
           gi_vmem, put_sem, x_ref, wf, wg, wm, adj, gall, asend, arecv, afull, bmat, direct, acc, hid, f1, f2, actcot, part, table,
           *rest):
    scratch = [rest[9 * i:9 * i + 9] for i in range(3)]
    local_sem, ring_send, ring_recv, sib_send, sib_recv, adj_send, adj_recv = rest[27:34]
    sems = [rest[34 + 2 * i:36 + 2 * i] for i in range(3)]
    p = Place(Y, Z)
    R = 2 * Z
    per_tile = nbr.shape[0]
    entries = 2 * per_tile
    rows = TILE // X
    sends = []

    def fetch(i, src, dst):
        item = pltpu.make_async_copy(src, dst, local_sem.at[i])
        item.start()
        return item

    get_cot = [fetch(t, cot_hbm.at[t], gall.at[t, p.region]) for t in range(2)]
    get_adj = fetch(2, adj_hbm, adj)
    get_x = fetch(3, x_hbm, x_ref)
    get_wf = fetch(4, wf_hbm, wf)
    get_wg = fetch(5, wg_hbm, wg)
    get_wm = fetch(6, wm_hbm, wm)

    barrier = pltpu.get_barrier_semaphore()
    partners = [(p.dp, lax.rem(p.region + i, R)) for i in range(1, R)]
    partners += [p.along(axis, i) for axis, n in (("x", X), ("y", Y)) for i in range(1, n)]
    for device in partners:
        pl.semaphore_signal(barrier, inc=1, device_id=device, device_id_type=MESH)

    def remote(src, dst, send, recv, device):
        item = pltpu.make_async_remote_copy(
            src_ref=src, dst_ref=dst, send_sem=send, recv_sem=recv, device_id=device, device_id_type=MESH)
        item.start()
        sends.append(item)

    def arrived(ref, send, recv):
        pltpu.make_async_remote_copy(
            src_ref=ref, dst_ref=ref, send_sem=send, recv_sem=recv, device_id=p.sibling, device_id_type=MESH
        ).wait_recv()

    def origin(direction, step):
        return lax.rem(p.at["z"] + (Z - step if direction == 0 else step), Z)

    def ring(step):
        for t in range(2):
            for direction in range(2):
                reach = Z // 2 if t == direction else Z // 2 - 1
                if step > reach:
                    continue
                slot = origin(direction, step) * 2 + p.c
                for tile in range(2):
                    block = gall.at[t, slot, pl.ds(tile * TILE, TILE)]
                    if step > 0:
                        arrived(block, ring_send.at[direction, t, step - 1, tile],
                                ring_recv.at[direction, t, step - 1, tile])
                    if step < reach:
                        remote(block, block, ring_send.at[direction, t, step, tile],
                               ring_recv.at[direction, t, step, tile], p.along("z", 1 if direction == 0 else Z - 1))
                if step > 0 or direction == 0:
                    block = gall.at[t, slot]
                    remote(block, block, sib_send.at[direction, t, step], sib_recv.at[direction, t, step], p.sibling)

    def scan(region, carry):
        entry = valid = other = mine = jnp.int32(0)
        for e in range(entries):
            a = nbr[e % per_tile, p.region * 2 + e // per_tile]
            hit = lax.div(a, 2) == region
            entry = jnp.where(hit, e, entry)
            valid = jnp.where(hit, 1, valid)
            b = nbr[e % per_tile, region * 2 + e // per_tile]
            back = lax.div(b, 2) == p.region
            other = jnp.where(back, e // per_tile, other)
            mine = jnp.where(back, lax.rem(b, 2), mine)
        for row, value in enumerate((entry, valid, other, mine)):
            table[row, region] = value
        return carry

    def fill(region, carry):
        block = adj[table[0, region], pl.ds(pl.multiple_of(p.at["x"] * rows, rows), rows)]
        asend[region] = jnp.where(table[1, region] == 1, block, jnp.zeros_like(block))
        return carry

    def forward(t):
        pre_f = dot(x_ref[t], wf[0], (1, 0))
        pre_g = dot(x_ref[t], wg[0], (1, 0))
        if t == 1:
            pre_f = pre_f + dot(x_ref[0], wf[1], (1, 0))
            pre_g = pre_g + dot(x_ref[0], wg[1], (1, 0))
        filt = jnp.tanh(pre_f)
        gate = jax.nn.sigmoid(pre_g)
        both = filt * gate
        hid[t] = both.astype(BF16)
        f1[t] = gate * (1.0 - filt * filt)
        f2[t] = both * (1.0 - gate)

    def own_products():
        for t in range(2):
            cot = gall[t, p.region]
            direct[t] = dot(cot, wm[0], (1, 1))
            here = dot(hid[t], cot, (0, 0))
            part[0] = here if t == 0 else part[0] + here

    def send_adjacency():
        arecv[p.region] = asend[p.region]
        for i in range(1, R):
            target = lax.rem(p.region + i, R)
            remote(asend.at[target], arecv.at[p.region], adj_send.at[i], adj_recv.at[i], (p.dp, target))

    def share_adjacency():
        for i in range(1, R):
            source = lax.rem(p.region + R - i, R)
            arrived(arecv.at[source], adj_send.at[i], adj_recv.at[i])
        for i in range(1, X):
            remote(arecv, afull.at[p.at["x"]], adj_send.at[R + i], adj_recv.at[R + i], p.along("x", i))
        afull[p.at["x"]] = arecv[...]

    def wait_adjacency():
        for i in range(1, X):
            source = lax.rem(p.at["x"] + X - i, X)
            arrived(afull.at[source], adj_send.at[R + i], adj_recv.at[R + i])

    def build(chip, carry):
        for core in range(2):
            region = chip * 2 + core
            block = afull[:, region].reshape(TILE, TILE).T
            zero = jnp.zeros_like(block)
            for j in range(2):
                bmat[chip, j * TILE:(j + 1) * TILE, core * TILE:(core + 1) * TILE] = jnp.where(
                    table[3, region] == j, block, zero)
        return carry

    def gathered(step):
        for t in range(2):
            for direction in range(2):
                if step > (Z // 2 if t == direction else Z // 2 - 1) or (step == 0 and direction == 1):
                    continue
                chip = origin(direction, step)
                arrived(gall.at[t, chip * 2 + 1 - p.c], sib_send.at[direction, t, step], sib_recv.at[direction, t, step])
                halves = []
                for core in range(2):
                    region = chip * 2 + core
                    halves.append(jnp.where(table[2, region] == 0, gall[t, region, :TILE], gall[t, region, TILE:]))
                more = dot(bmat[chip], jnp.concatenate(halves, axis=0), (1, 0))
                acc[t] = more if step == 0 else acc[t] + more

    lax.fori_loop(0, R, scan, 0)
    get_adj.wait()
    lax.fori_loop(0, R, fill, 0)
    for item in (get_x, get_wf, get_wg, *get_cot):
        item.wait()
    forward(0)
    pl.semaphore_wait(barrier, len(partners))
    send_adjacency()
    ring(0)
    forward(1)
    ring(1)
    get_wm.wait()
    own_products()
    for step in range(2, Z // 2 + 1):
        ring(step)
        if step == 2:
            share_adjacency()
    wait_adjacency()
    lax.fori_loop(0, Z, build, 0)
    for step in range(Z // 2 + 1):
        gathered(step)

    groups = [
        Reduction(p, order, part, 2 * i, factor, scratch[i], sems[i], sends) for i, order in enumerate(ORDERS)
    ]
    mixed = [acc[t].astype(BF16) for t in range(2)]
    part[1] = dot(hid[0], mixed[0], (0, 0)) + dot(hid[1], mixed[1], (0, 0))
    groups[0].start_core()
    for t in range(2):
        grad = direct[t] + dot(mixed[t], wm[1], (1, 1))
        actcot[0, t] = (grad * f1[t]).astype(BF16)
        actcot[1, t] = (grad * f2[t]).astype(BF16)
    for g in range(2):
        part[2 + 2 * g] = dot(x_ref[0], actcot[g, 0], (0, 0)) + dot(x_ref[1], actcot[g, 1], (0, 0))
        part[3 + 2 * g] = dot(x_ref[0], actcot[g, 1], (0, 0))
        groups[1 + g].start_core()
    late, also, early = groups
    for group in groups:
        group.start_first()
    for t in range(2):
        total = gall[t, p.region].astype(F32)
        for tap in range(2 - t):
            total = total + dot(actcot[0, t + tap], wf[tap], (1, 1)) + dot(actcot[1, t + tap], wg[tap], (1, 1))
        gi_vmem[t] = total.astype(BF16)
    puts = [pltpu.make_async_copy(gi_vmem, gi_ref, local_sem.at[7])]
    puts[0].start()
    for stage in ("start_second", "start_third", "start_gather_second"):
        for group in (early, late, also):
            getattr(group, stage)()
    for group in (late, also, early):
        group.start_gather_first()
    for group in (early, late, also):
        group.start_gather_core()
    outs = [out_mix, out_filter, out_gate]
    for group in (early, late, also):
        puts += group.put(outs[groups.index(group)], put_sem, 0)
    for group in (early, late, also):
        group.wait()
        puts += group.put(outs[groups.index(group)], put_sem, 1)
    for item in puts:
        item.wait()
    for item in sends:
        item.wait_send()


def write(gi, mix, filt, gate, gi_out, mix_out, filt_out, gate_out, wide, sem):
    copies = [pltpu.make_async_copy(gi, gi_out, sem.at[3])]
    copies[0].start()
    for i, (source, out) in enumerate(((mix, mix_out), (filt, filt_out), (gate, gate_out))):
        wide[i] = source[...].astype(F32)
        copies.append(pltpu.make_async_copy(wide.at[i], out, sem.at[i]))
        copies[-1].start()
    for item in copies:
        item.wait()


def reduction_scratch(order, chans, sizes):
    n1, n2, n3 = (sizes[axis] for axis in order)
    each = 2 * (TILE // n1 // 8) * (chans // 128) // n2
    return [
        pltpu.VMEM((2, TILE, chans), F32),
        pltpu.VMEM((n1, 2, TILE // n1, chans), BF16),
        pltpu.VMEM((n1 - 1, 2, TILE // n1, chans), BF16),
        pltpu.VMEM((n2, each, 8, 128), F32),
        pltpu.VMEM((n2 - 1, each, 8, 128), F32),
        pltpu.VMEM((n3, each, 8, 128), F32),
        pltpu.VMEM((n2, each, 8, 128), F32),
        pltpu.VMEM((n1, 2, TILE // n1, chans), BF16),
        pltpu.VMEM((n1, 2, TILE // n1, chans), BF16),
    ]


def solution(mesh):
    Y, Z = mesh.shape["dp"] // X, mesh.shape["region"] // 2
    R = 2 * Z
    sizes = {"x": X, "y": Y, "z": Z}

    def per_device(inputs, cotangent, w_filter, w_gate, w_mix, neighbours, adjacency):
        _, steps, sites, chans = inputs.shape
        total_rows = steps * sites * mesh.shape["dp"] * R
        per_tile = neighbours.shape[1]
        dma = pltpu.SemaphoreType.DMA
        vmem = pl.BlockSpec(memory_space=pltpu.VMEM)
        hbm = pl.BlockSpec(memory_space=pltpu.HBM)
        scratch, sems = [], []
        for order in ORDERS:
            scratch += reduction_scratch(order, chans, sizes)
            n1, n2, n3 = (sizes[axis] for axis in order)
            count = 2 + 2 * (n1 - 1) + 2 * (n2 - 1) + n3 - 1
            sems += [dma((count,)), dma((count,))]
        weights = pltpu.VMEM((2, chans, chans), BF16)
        wide = pltpu.VMEM((steps, sites, chans), F32)
        narrow = pltpu.VMEM((steps, sites, chans), BF16)
        shapes = [(2, 2, sizes[order[0]], TILE // sizes[order[0]], chans) for order in ORDERS]
        grad_inputs, *grads = pl.pallas_call(
            functools.partial(kernel, Y, Z, 1.0 / math.sqrt(total_rows)),
            out_shape=[
                jax.ShapeDtypeStruct(shape, BF16) for shape in [(steps, sites, chans), *shapes]
            ],
            in_specs=[pl.BlockSpec(memory_space=pltpu.SMEM)] + [hbm] * 6,
            out_specs=[hbm] * 4,
            scratch_shapes=[
                narrow, dma((2, 6)), narrow, weights, weights, weights,
                pltpu.VMEM((2 * per_tile, TILE, TILE), BF16),
                pltpu.VMEM((steps, R, sites, chans), BF16),
                pltpu.VMEM((R, TILE // X, TILE), BF16),
                pltpu.VMEM((R, TILE // X, TILE), BF16),
                pltpu.VMEM((X, R, TILE // X, TILE), BF16),
                pltpu.VMEM((Z, 2 * TILE, 2 * TILE), BF16),
                wide, wide, narrow, wide, wide,
                pltpu.VMEM((2, steps, sites, chans), BF16),
                pltpu.VMEM((6, chans, chans), F32),
                pltpu.SMEM((4, R), jnp.int32),
                *scratch,
                dma((8,)),
                dma((2, 2, Z // 2, 2)), dma((2, 2, Z // 2, 2)),
                dma((2, 2, Z // 2 + 1)), dma((2, 2, Z // 2 + 1)),
                dma((R + X,)), dma((R + X,)),
                *sems,
            ],
            compiler_params=pltpu.CompilerParams(
                collective_id=0, has_side_effects=True, vmem_limit_bytes=56 << 20),
            name="train_step",
        )(neighbours.T, inputs[0], cotangent[0], w_filter, w_gate, w_mix,
          adjacency.reshape(2 * per_tile, TILE, TILE))
        grad = jax.ShapeDtypeStruct((2, chans, chans), F32)
        grad_inputs, grad_mix, grad_filter, grad_gate = pl.pallas_call(
            write,
            out_shape=(jax.ShapeDtypeStruct((steps, sites, chans), BF16), grad, grad, grad),
            in_specs=[vmem] * 4,
            out_specs=(hbm,) * 4,
            scratch_shapes=[pltpu.VMEM((3, 2, chans, chans), F32), dma((4,))],
            name="write",
        )(grad_inputs, *[block.reshape(2, chans, chans) for block in grads])
        return grad_inputs[None], grad_filter, grad_gate, grad_mix

    return jax.shard_map(
        per_device,
        mesh=mesh,
        in_specs=(
            P("dp", None, "region", None),
            P("dp", None, "region", None),
            P(),
            P(),
            P(),
            P(),
            P("region", None, None, None),
        ),
        out_specs=(P("dp", None, "region", None), P(), P(), P()),
        check_vma=False,
    )
```

```python
import functools
import itertools
import math

import jax
import jax.numpy as jnp
from jax import lax
from jax.experimental import pallas as pl
from jax.experimental.pallas import tpu as pltpu
from jax.sharding import PartitionSpec as P

MESH = pl.DeviceIdType.MESH
X = 4
TILE = 128
ORDERS = ("yxz", "zxy", "xzy")
F32 = jnp.float32
BF16 = jnp.bfloat16


def dot(a, b, contract):
    return lax.dot_general(a, b, ((contract[:1], contract[1:]), ((), ())), preferred_element_type=F32)


class Place:
    def __init__(self, Y, Z):
        self.size = {"x": X, "y": Y, "z": Z}
        self.dp = lax.axis_index("dp")
        self.region = lax.axis_index("region")
        self.at = {
            "x": lax.div(self.dp, Y), "y": lax.rem(self.dp, Y), "z": lax.div(self.region, 2),
        }
        self.c = lax.rem(self.region, 2)
        self.sibling = (self.dp, self.at["z"] * 2 + 1 - self.c)

    def along(self, axis, i):
        at = dict(self.at)
        at[axis] = lax.rem(at[axis] + i, self.size[axis])
        return (at["x"] * self.size["y"] + at["y"], at["z"] * 2 + self.c)


class Reduction:
    def __init__(self, place, order, part, base, factor, scratch, sems, sends):
        self.p, self.order, self.part, self.base, self.factor, self.sends = place, order, part, base, factor, sends
        self.core, self.s1, self.r1, self.s2, self.r2, self.x3, self.g2, self.g1, self.cg = scratch
        self.send, self.recv = sems
        self.items, self.used = [], 0

    def copy(self, src, dst, device):
        item = pltpu.make_async_remote_copy(
            src_ref=src, dst_ref=dst, send_sem=self.send.at[self.used], recv_sem=self.recv.at[self.used],
            device_id=device, device_id_type=MESH,
        )
        self.used += 1
        item.start()
        self.sends.append(item)
        self.items.append(item)

    def wait(self):
        for item in self.items:
            item.wait_recv()
        self.items = []

    def peers(self, k):
        axis = self.order[k]
        n, at = self.p.size[axis], self.p.at[axis]
        return n, at, [(i, lax.rem(at + i, n), self.p.along(axis, i)) for i in range(1, n)]

    def start_core(self):
        other = pl.ds(pl.multiple_of((1 - self.p.c) * TILE, TILE), TILE)
        self.copy(self.part.at[pl.ds(self.base, 2), other], self.core, self.p.sibling)

    def start_first(self):
        self.wait()
        n, at, peers = self.peers(0)
        mine = pl.ds(pl.multiple_of(self.p.c * TILE, TILE), TILE)
        for i in range(2):
            total = self.core[i] + self.part[self.base + i, mine]
            self.core[i] = total
            self.s1[:, i] = total.astype(BF16).reshape(n, TILE // n, total.shape[-1])
        for i, slot, device in peers:
            self.copy(self.s1.at[slot], self.r1.at[i - 1], device)

    def start_second(self):
        self.wait()
        first, at, _ = self.peers(0)
        rows = TILE // first
        tiles = []
        for i in range(2):
            total = self.core[i, pl.ds(pl.multiple_of(at * rows, rows), rows)]
            for j in range(first - 1):
                total = total + self.r1[j, i].astype(F32)
            tiles += [
                total[r * 8:r * 8 + 8, h * 128:h * 128 + 128] for r in range(rows // 8) for h in range(2)
            ]
        n, at, peers = self.peers(1)
        each = len(tiles) // n
        for index, tile in enumerate(tiles):
            self.s2[index // each, index % each] = tile
        for i, slot, device in peers:
            self.copy(self.s2.at[slot], self.r2.at[i - 1], device)

    def start_third(self):
        self.wait()
        n, at, _ = self.peers(1)
        total = self.s2[at]
        for j in range(n - 1):
            total = total + self.r2[j]
        n, at, peers = self.peers(2)
        self.x3[at] = total
        for i, slot, device in peers:
            self.copy(self.x3.at[at], self.x3.at[at], device)

    def start_gather_second(self):
        self.wait()
        total = self.x3[0]
        for j in range(1, self.peers(2)[0]):
            total = total + self.x3[j]
        n, at, peers = self.peers(1)
        self.g2[at] = total * self.factor
        for i, slot, device in peers:
            self.copy(self.g2.at[at], self.g2.at[at], device)

    def start_gather_first(self):
        self.wait()
        n, at, peers = self.peers(0)
        each = self.g2.shape[1]
        tiles = [self.g2[i, j] for i in range(self.g2.shape[0]) for j in range(each)]
        for i in range(2):
            mine = tiles[i * len(tiles) // 2:(i + 1) * len(tiles) // 2]
            rows = [jnp.concatenate(mine[r:r + 2], axis=1) for r in range(0, len(mine), 2)]
            self.g1[at, i] = jnp.concatenate(rows, axis=0).astype(BF16)
        for i, slot, device in peers:
            self.copy(self.g1.at[at], self.g1.at[at], device)

    def start_gather_core(self):
        self.wait()
        self.copy(self.g1, self.cg, self.p.sibling)

    def put(self, out, sem, other):
        source, core = (self.cg, 1 - self.p.c) if other else (self.g1, self.p.c)
        copies = [
            pltpu.make_async_copy(source.at[:, i], out.at[i, core], sem.at[other, self.base + i]) for i in range(2)
        ]
        for item in copies:
            item.start()
        return copies


def kernel(Y, Z, factor, nbr, x_hbm, cot_hbm, wf_hbm, wg_hbm, wm_hbm, adj_hbm,
           gi_ref, out_mix, out_filter, out_gate,
           gi_vmem, put_sem, x_ref, wf, wg, wm, adj, gall, asend, arecv, apair, afull, bmat, direct, acc, hid, f1, f2, actcot, part, table,
           *rest):
    scratch = [rest[9 * i:9 * i + 9] for i in range(3)]
    local_sem, ring_send, ring_recv, sib_send, sib_recv, adj_send, adj_recv = rest[27:34]
    sems = [rest[34 + 2 * i:36 + 2 * i] for i in range(3)]
    p = Place(Y, Z)
    R = 2 * Z
    per_tile = nbr.shape[0]
    entries = 2 * per_tile
    rows = TILE // (2 * X)
    parity = lax.rem(p.at["y"], 2)
    sends = []

    def fetch(i, src, dst):
        item = pltpu.make_async_copy(src, dst, local_sem.at[i])
        item.start()
        return item

    get_cot = [fetch(t, cot_hbm.at[t], gall.at[t, p.region]) for t in range(2)]
    get_adj = fetch(2, adj_hbm, adj)
    get_x = fetch(3, x_hbm, x_ref)
    get_wf = fetch(4, wf_hbm, wf)
    get_wg = fetch(5, wg_hbm, wg)
    get_wm = fetch(6, wm_hbm, wm)

    barrier = pltpu.get_barrier_semaphore()
    partners = [(p.dp, lax.rem(p.region + i, R)) for i in range(1, R)]
    partners += [p.along(axis, i) for axis, n in (("x", X), ("y", Y)) for i in range(1, n)]
    for device in partners:
        pl.semaphore_signal(barrier, inc=1, device_id=device, device_id_type=MESH)

    def remote(src, dst, send, recv, device):
        item = pltpu.make_async_remote_copy(
            src_ref=src, dst_ref=dst, send_sem=send, recv_sem=recv, device_id=device, device_id_type=MESH)
        item.start()
        sends.append(item)

    def arrived(ref, send, recv):
        pltpu.make_async_remote_copy(
            src_ref=ref, dst_ref=ref, send_sem=send, recv_sem=recv, device_id=p.sibling, device_id_type=MESH
        ).wait_recv()

    def origin(direction, step):
        return lax.rem(p.at["z"] + (Z - step if direction == 0 else step), Z)

    def ring(step, times=(0, 1)):
        for t, tile, direction in itertools.product(times, range(2), range(2)):
            reach = Z // 2 if t == direction else Z // 2 - 1
            if step > reach:
                continue
            block = gall.at[t, origin(direction, step) * 2 + p.c, pl.ds(tile * TILE, TILE)]
            if step > 0:
                arrived(block, ring_send.at[direction, t, step - 1, tile], ring_recv.at[direction, t, step - 1, tile])
            if step < reach:
                remote(block, block, ring_send.at[direction, t, step, tile], ring_recv.at[direction, t, step, tile],
                       p.along("z", 1 if direction == 0 else Z - 1))
            if step > 0 or direction == 0:
                remote(block, block, sib_send.at[direction, t, step, tile], sib_recv.at[direction, t, step, tile],
                       p.sibling)

    def scan(region, carry):
        entry = valid = other = mine = jnp.int32(0)
        for e in range(entries):
            a = nbr[e % per_tile, p.region * 2 + e // per_tile]
            hit = lax.div(a, 2) == region
            entry = jnp.where(hit, e, entry)
            valid = jnp.where(hit, 1, valid)
            b = nbr[e % per_tile, region * 2 + e // per_tile]
            back = lax.div(b, 2) == p.region
            other = jnp.where(back, e // per_tile, other)
            mine = jnp.where(back, lax.rem(b, 2), mine)
        for row, value in enumerate((entry, valid, other, mine)):
            table[row, region] = value
        return carry

    def fill(region, carry):
        block = adj[table[0, region], pl.ds(pl.multiple_of((p.at["x"] * 2 + parity) * rows, rows), rows)]
        asend[region] = jnp.where(table[1, region] == 1, block, jnp.zeros_like(block))
        return carry

    def forward(t):
        pre_f = dot(x_ref[t], wf[0], (1, 0))
        pre_g = dot(x_ref[t], wg[0], (1, 0))
        if t == 1:
            pre_f = pre_f + dot(x_ref[0], wf[1], (1, 0))
            pre_g = pre_g + dot(x_ref[0], wg[1], (1, 0))
        filt = jnp.tanh(pre_f)
        gate = jax.nn.sigmoid(pre_g)
        both = filt * gate
        hid[t] = both.astype(BF16)
        f1[t] = gate * (1.0 - filt * filt)
        f2[t] = both * (1.0 - gate)

    def own_products():
        for t in range(2):
            cot = gall[t, p.region]
            direct[t] = dot(cot, wm[0], (1, 1))
            here = dot(hid[t], cot, (0, 0))
            part[0] = here if t == 0 else part[0] + here

    def send_adjacency():
        arecv[p.region] = asend[p.region]
        for i in range(1, R):
            target = lax.rem(p.region + i, R)
            remote(asend.at[target], arecv.at[p.region], adj_send.at[i], adj_recv.at[i], (p.dp, target))

    def pair_adjacency():
        for i in range(1, R):
            source = lax.rem(p.region + R - i, R)
            arrived(arecv.at[source], adj_send.at[i], adj_recv.at[i])
        remote(arecv, apair.at[parity], adj_send.at[R + X], adj_recv.at[R + X], p.along("y", 1 + (Y - 2) * parity))
        apair[parity] = arecv[...]

    def share_adjacency():
        arrived(apair.at[1 - parity], adj_send.at[R + X], adj_recv.at[R + X])
        for i in range(1, X):
            remote(apair, afull.at[p.at["x"]], adj_send.at[R + i], adj_recv.at[R + i], p.along("x", i))
        afull[p.at["x"]] = apair[...]

    def wait_adjacency():
        for i in range(1, X):
            source = lax.rem(p.at["x"] + X - i, X)
            arrived(afull.at[source], adj_send.at[R + i], adj_recv.at[R + i])

    def build(chip, carry):
        for core in range(2):
            region = chip * 2 + core
            block = afull[:, :, region].reshape(TILE, TILE).T
            zero = jnp.zeros_like(block)
            for j in range(2):
                bmat[chip, j * TILE:(j + 1) * TILE, core * TILE:(core + 1) * TILE] = jnp.where(
                    table[3, region] == j, block, zero)
        return carry

    def gathered(step):
        for t in range(2):
            for direction in range(2):
                if step > (Z // 2 if t == direction else Z // 2 - 1) or (step == 0 and direction == 1):
                    continue
                chip = origin(direction, step)
                for tile in range(2):
                    arrived(gall.at[t, chip * 2 + 1 - p.c, pl.ds(tile * TILE, TILE)],
                            sib_send.at[direction, t, step, tile], sib_recv.at[direction, t, step, tile])
                halves = []
                for core in range(2):
                    region = chip * 2 + core
                    halves.append(jnp.where(table[2, region] == 0, gall[t, region, :TILE], gall[t, region, TILE:]))
                more = dot(bmat[chip], jnp.concatenate(halves, axis=0), (1, 0))
                acc[t] = more if step == 0 else acc[t] + more

    lax.fori_loop(0, R, scan, 0)
    get_adj.wait()
    lax.fori_loop(0, R, fill, 0)
    for item in get_cot:
        item.wait()
    pl.semaphore_wait(barrier, len(partners))
    ring(0, (0,))
    send_adjacency()
    ring(0, (1,))
    for item in (get_x, get_wf, get_wg):
        item.wait()
    forward(0)
    forward(1)
    pair_adjacency()
    ring(1)
    share_adjacency()
    get_wm.wait()
    own_products()
    for step in range(2, Z // 2):
        ring(step)
    wait_adjacency()
    lax.fori_loop(0, Z, build, 0)
    for step in range(Z // 2 - 1):
        gathered(step)
    ring(Z // 2)
    gathered(Z // 2 - 1)
    gathered(Z // 2)

    groups = [
        Reduction(p, order, part, 2 * i, factor, scratch[i], sems[i], sends) for i, order in enumerate(ORDERS)
    ]
    mixed = [acc[t].astype(BF16) for t in range(2)]
    part[1] = dot(hid[0], mixed[0], (0, 0)) + dot(hid[1], mixed[1], (0, 0))
    groups[0].start_core()
    for t in range(2):
        grad = direct[t] + dot(mixed[t], wm[1], (1, 1))
        actcot[0, t] = (grad * f1[t]).astype(BF16)
        actcot[1, t] = (grad * f2[t]).astype(BF16)
    for g in range(2):
        part[2 + 2 * g] = dot(x_ref[0], actcot[g, 0], (0, 0)) + dot(x_ref[1], actcot[g, 1], (0, 0))
        part[3 + 2 * g] = dot(x_ref[0], actcot[g, 1], (0, 0))
        groups[1 + g].start_core()
    late, also, early = groups
    for group in groups:
        group.start_first()
    for t in range(2):
        total = gall[t, p.region].astype(F32)
        for tap in range(2 - t):
            total = total + dot(actcot[0, t + tap], wf[tap], (1, 1)) + dot(actcot[1, t + tap], wg[tap], (1, 1))
        gi_vmem[t] = total.astype(BF16)
    puts = [pltpu.make_async_copy(gi_vmem, gi_ref, local_sem.at[7])]
    puts[0].start()
    for stage in ("start_second", "start_third", "start_gather_second"):
        for group in (early, late, also):
            getattr(group, stage)()
    for group in (late, also, early):
        group.start_gather_first()
    for group in (early, late, also):
        group.start_gather_core()
    outs = [out_mix, out_filter, out_gate]
    for group in (early, late, also):
        puts += group.put(outs[groups.index(group)], put_sem, 0)
    for group in (early, late, also):
        group.wait()
        puts += group.put(outs[groups.index(group)], put_sem, 1)
    for item in puts:
        item.wait()
    for item in sends:
        item.wait_send()


def write(gi, mix, filt, gate, gi_out, mix_out, filt_out, gate_out, wide, sem):
    copies = [pltpu.make_async_copy(gi, gi_out, sem.at[3])]
    copies[0].start()
    for i, (source, out) in enumerate(((mix, mix_out), (filt, filt_out), (gate, gate_out))):
        wide[i] = source[...].astype(F32)
        copies.append(pltpu.make_async_copy(wide.at[i], out, sem.at[i]))
        copies[-1].start()
    for item in copies:
        item.wait()


def reduction_scratch(order, chans, sizes):
    n1, n2, n3 = (sizes[axis] for axis in order)
    each = 2 * (TILE // n1 // 8) * (chans // 128) // n2
    return [
        pltpu.VMEM((2, TILE, chans), F32),
        pltpu.VMEM((n1, 2, TILE // n1, chans), BF16),
        pltpu.VMEM((n1 - 1, 2, TILE // n1, chans), BF16),
        pltpu.VMEM((n2, each, 8, 128), F32),
        pltpu.VMEM((n2 - 1, each, 8, 128), F32),
        pltpu.VMEM((n3, each, 8, 128), F32),
        pltpu.VMEM((n2, each, 8, 128), F32),
        pltpu.VMEM((n1, 2, TILE // n1, chans), BF16),
        pltpu.VMEM((n1, 2, TILE // n1, chans), BF16),
    ]


def solution(mesh):
    Y, Z = mesh.shape["dp"] // X, mesh.shape["region"] // 2
    R = 2 * Z
    sizes = {"x": X, "y": Y, "z": Z}

    def per_device(inputs, cotangent, w_filter, w_gate, w_mix, neighbours, adjacency):
        _, steps, sites, chans = inputs.shape
        total_rows = steps * sites * mesh.shape["dp"] * R
        per_tile = neighbours.shape[1]
        dma = pltpu.SemaphoreType.DMA
        vmem = pl.BlockSpec(memory_space=pltpu.VMEM)
        hbm = pl.BlockSpec(memory_space=pltpu.HBM)
        scratch, sems = [], []
        for order in ORDERS:
            scratch += reduction_scratch(order, chans, sizes)
            n1, n2, n3 = (sizes[axis] for axis in order)
            count = 2 + 2 * (n1 - 1) + 2 * (n2 - 1) + n3 - 1
            sems += [dma((count,)), dma((count,))]
        weights = pltpu.VMEM((2, chans, chans), BF16)
        wide = pltpu.VMEM((steps, sites, chans), F32)
        narrow = pltpu.VMEM((steps, sites, chans), BF16)
        shapes = [(2, 2, sizes[order[0]], TILE // sizes[order[0]], chans) for order in ORDERS]
        grad_inputs, *grads = pl.pallas_call(
            functools.partial(kernel, Y, Z, 1.0 / math.sqrt(total_rows)),
            out_shape=[
                jax.ShapeDtypeStruct(shape, BF16) for shape in [(steps, sites, chans), *shapes]
            ],
            in_specs=[pl.BlockSpec(memory_space=pltpu.SMEM)] + [hbm] * 6,
            out_specs=[hbm] * 4,
            scratch_shapes=[
                narrow, dma((2, 6)), narrow, weights, weights, weights,
                pltpu.VMEM((2 * per_tile, TILE, TILE), BF16),
                pltpu.VMEM((steps, R, sites, chans), BF16),
                pltpu.VMEM((R, TILE // (2 * X), TILE), BF16),
                pltpu.VMEM((R, TILE // (2 * X), TILE), BF16),
                pltpu.VMEM((2, R, TILE // (2 * X), TILE), BF16),
                pltpu.VMEM((X, 2, R, TILE // (2 * X), TILE), BF16),
                pltpu.VMEM((Z, 2 * TILE, 2 * TILE), BF16),
                wide, wide, narrow, wide, wide,
                pltpu.VMEM((2, steps, sites, chans), BF16),
                pltpu.VMEM((6, chans, chans), F32),
                pltpu.SMEM((4, R), jnp.int32),
                *scratch,
                dma((8,)),
                dma((2, 2, Z // 2, 2)), dma((2, 2, Z // 2, 2)),
                dma((2, 2, Z // 2 + 1, 2)), dma((2, 2, Z // 2 + 1, 2)),
                dma((R + X + 1,)), dma((R + X + 1,)),
                *sems,
            ],
            compiler_params=pltpu.CompilerParams(
                collective_id=0, has_side_effects=True, vmem_limit_bytes=56 << 20),
            name="train_step",
        )(neighbours.T, inputs[0], cotangent[0], w_filter, w_gate, w_mix,
          adjacency.reshape(2 * per_tile, TILE, TILE))
        grad = jax.ShapeDtypeStruct((2, chans, chans), F32)
        grad_inputs, grad_mix, grad_filter, grad_gate = pl.pallas_call(
            write,
            out_shape=(jax.ShapeDtypeStruct((steps, sites, chans), BF16), grad, grad, grad),
            in_specs=[vmem] * 4,
            out_specs=(hbm,) * 4,
            scratch_shapes=[pltpu.VMEM((3, 2, chans, chans), F32), dma((4,))],
            name="write",
        )(grad_inputs, *[block.reshape(2, chans, chans) for block in grads])
        return grad_inputs[None], grad_filter, grad_gate, grad_mix

    return jax.shard_map(
        per_device,
        mesh=mesh,
        in_specs=(
            P("dp", None, "region", None),
            P("dp", None, "region", None),
            P(),
            P(),
            P(),
            P(),
            P("region", None, None, None),
        ),
        out_specs=(P("dp", None, "region", None), P(), P(), P()),
        check_vma=False,
    )
```

```python
import functools
import itertools
import math

import jax
import jax.numpy as jnp
from jax import lax
from jax.experimental import pallas as pl
from jax.experimental.pallas import tpu as pltpu
from jax.sharding import PartitionSpec as P

MESH = pl.DeviceIdType.MESH
X = 4
TILE = 128
ORDERS = ("yxz", "zxy", "xzy")
F32 = jnp.float32
BF16 = jnp.bfloat16


def dot(a, b, contract):
    return lax.dot_general(a, b, ((contract[:1], contract[1:]), ((), ())), preferred_element_type=F32)


class Place:
    def __init__(self, Y, Z):
        self.size = {"x": X, "y": Y, "z": Z}
        self.dp = lax.axis_index("dp")
        self.region = lax.axis_index("region")
        self.at = {
            "x": lax.div(self.dp, Y), "y": lax.rem(self.dp, Y), "z": lax.div(self.region, 2),
        }
        self.c = lax.rem(self.region, 2)
        self.sibling = (self.dp, self.at["z"] * 2 + 1 - self.c)

    def along(self, axis, i):
        at = dict(self.at)
        at[axis] = lax.rem(at[axis] + i, self.size[axis])
        return (at["x"] * self.size["y"] + at["y"], at["z"] * 2 + self.c)


class Reduction:
    def __init__(self, place, order, part, base, factor, scratch, sems, sends):
        self.p, self.order, self.part, self.base, self.factor, self.sends = place, order, part, base, factor, sends
        self.core, self.s1, self.r1, self.s2, self.r2, self.x3, self.g2, self.g1, self.cg = scratch
        self.send, self.recv = sems
        self.items, self.used = [], 0

    def copy(self, src, dst, device):
        item = pltpu.make_async_remote_copy(
            src_ref=src, dst_ref=dst, send_sem=self.send.at[self.used], recv_sem=self.recv.at[self.used],
            device_id=device, device_id_type=MESH,
        )
        self.used += 1
        item.start()
        self.sends.append(item)
        self.items.append(item)

    def wait(self):
        for item in self.items:
            item.wait_recv()
        self.items = []

    def peers(self, k):
        axis = self.order[k]
        n, at = self.p.size[axis], self.p.at[axis]
        return n, at, [(i, lax.rem(at + i, n), self.p.along(axis, i)) for i in range(1, n)]

    def start_core(self):
        other = pl.ds(pl.multiple_of((1 - self.p.c) * TILE, TILE), TILE)
        self.copy(self.part.at[pl.ds(self.base, 2), other], self.core, self.p.sibling)

    def start_first(self):
        self.wait()
        n, at, peers = self.peers(0)
        mine = pl.ds(pl.multiple_of(self.p.c * TILE, TILE), TILE)
        for i in range(2):
            total = self.core[i] + self.part[self.base + i, mine]
            self.core[i] = total
            self.s1[:, i] = total.astype(BF16).reshape(n, TILE // n, total.shape[-1])
        for i, slot, device in peers:
            self.copy(self.s1.at[slot], self.r1.at[i - 1], device)

    def start_second(self):
        self.wait()
        first, at, _ = self.peers(0)
        rows = TILE // first
        tiles = []
        for i in range(2):
            total = self.core[i, pl.ds(pl.multiple_of(at * rows, rows), rows)]
            for j in range(first - 1):
                total = total + self.r1[j, i].astype(F32)
            tiles += [
                total[r * 8:r * 8 + 8, h * 128:h * 128 + 128] for r in range(rows // 8) for h in range(2)
            ]
        n, at, peers = self.peers(1)
        each = len(tiles) // n
        for index, tile in enumerate(tiles):
            self.s2[index // each, index % each] = tile
        for i, slot, device in peers:
            self.copy(self.s2.at[slot], self.r2.at[i - 1], device)

    def start_third(self):
        self.wait()
        n, at, _ = self.peers(1)
        total = self.s2[at]
        for j in range(n - 1):
            total = total + self.r2[j]
        n, at, peers = self.peers(2)
        self.x3[at] = total
        for i, slot, device in peers:
            self.copy(self.x3.at[at], self.x3.at[at], device)

    def start_gather_second(self):
        self.wait()
        total = self.x3[0]
        for j in range(1, self.peers(2)[0]):
            total = total + self.x3[j]
        n, at, peers = self.peers(1)
        self.g2[at] = total * self.factor
        for i, slot, device in peers:
            self.copy(self.g2.at[at], self.g2.at[at], device)

    def start_gather_first(self):
        self.wait()
        n, at, peers = self.peers(0)
        each = self.g2.shape[1]
        tiles = [self.g2[i, j] for i in range(self.g2.shape[0]) for j in range(each)]
        for i in range(2):
            mine = tiles[i * len(tiles) // 2:(i + 1) * len(tiles) // 2]
            rows = [jnp.concatenate(mine[r:r + 2], axis=1) for r in range(0, len(mine), 2)]
            self.g1[at, i] = jnp.concatenate(rows, axis=0).astype(BF16)
        for i, slot, device in peers:
            self.copy(self.g1.at[at], self.g1.at[at], device)

    def start_gather_core(self):
        self.wait()
        self.copy(self.g1, self.cg, self.p.sibling)

    def put(self, out, sem, other):
        source, core = (self.cg, 1 - self.p.c) if other else (self.g1, self.p.c)
        copies = [
            pltpu.make_async_copy(source.at[:, i], out.at[i, core], sem.at[other, self.base + i]) for i in range(2)
        ]
        for item in copies:
            item.start()
        return copies


def kernel(Y, Z, factor, nbr, x_hbm, cot_hbm, wf_hbm, wg_hbm, wm_hbm, adj_hbm,
           gi_ref, out_mix, out_filter, out_gate,
           gi_vmem, put_sem, x_ref, wf, wg, wm, adj, gall, asend, arecv, apair, afull, bmat, direct, acc, hid, hid_t, x_t, wm_t, f1, f2, actcot, part, table,
           *rest):
    scratch = [rest[9 * i:9 * i + 9] for i in range(3)]
    local_sem, ring_send, ring_recv, sib_send, sib_recv, adj_send, adj_recv = rest[27:34]
    sems = [rest[34 + 2 * i:36 + 2 * i] for i in range(3)]
    p = Place(Y, Z)
    R = 2 * Z
    per_tile = nbr.shape[0]
    entries = 2 * per_tile
    rows = TILE // (2 * X)
    parity = lax.rem(p.at["y"], 2)
    sends = []

    def fetch(i, src, dst):
        item = pltpu.make_async_copy(src, dst, local_sem.at[i])
        item.start()
        return item

    get_cot = [fetch(t, cot_hbm.at[t], gall.at[t, p.region]) for t in range(2)]
    get_adj = fetch(2, adj_hbm, adj)
    get_x = fetch(3, x_hbm, x_ref)
    get_wf = fetch(4, wf_hbm, wf)
    get_wg = fetch(5, wg_hbm, wg)
    get_wm = fetch(6, wm_hbm, wm)

    barrier = pltpu.get_barrier_semaphore()
    partners = [(p.dp, lax.rem(p.region + i, R)) for i in range(1, R)]
    partners += [p.along(axis, i) for axis, n in (("x", X), ("y", Y)) for i in range(1, n)]
    for device in partners:
        pl.semaphore_signal(barrier, inc=1, device_id=device, device_id_type=MESH)

    def remote(src, dst, send, recv, device):
        item = pltpu.make_async_remote_copy(
            src_ref=src, dst_ref=dst, send_sem=send, recv_sem=recv, device_id=device, device_id_type=MESH)
        item.start()
        sends.append(item)

    def arrived(ref, send, recv):
        pltpu.make_async_remote_copy(
            src_ref=ref, dst_ref=ref, send_sem=send, recv_sem=recv, device_id=p.sibling, device_id_type=MESH
        ).wait_recv()

    def origin(direction, step):
        return lax.rem(p.at["z"] + (Z - step if direction == 0 else step), Z)

    def ring(step, times=(0, 1)):
        for t, tile, direction in itertools.product(times, range(2), range(2)):
            reach = Z // 2 if t == direction else Z // 2 - 1
            if step > reach:
                continue
            block = gall.at[t, origin(direction, step) * 2 + p.c, pl.ds(tile * TILE, TILE)]
            if step > 0:
                arrived(block, ring_send.at[direction, t, step - 1, tile], ring_recv.at[direction, t, step - 1, tile])
            if step < reach:
                remote(block, block, ring_send.at[direction, t, step, tile], ring_recv.at[direction, t, step, tile],
                       p.along("z", 1 if direction == 0 else Z - 1))
            if step > 0 or direction == 0:
                remote(block, block, sib_send.at[direction, t, step, tile], sib_recv.at[direction, t, step, tile],
                       p.sibling)

    def scan(region, carry):
        entry = valid = other = mine = jnp.int32(0)
        for e in range(entries):
            a = nbr[e % per_tile, p.region * 2 + e // per_tile]
            hit = lax.div(a, 2) == region
            entry = jnp.where(hit, e, entry)
            valid = jnp.where(hit, 1, valid)
            b = nbr[e % per_tile, region * 2 + e // per_tile]
            back = lax.div(b, 2) == p.region
            other = jnp.where(back, e // per_tile, other)
            mine = jnp.where(back, lax.rem(b, 2), mine)
        for row, value in enumerate((entry, valid, other, mine)):
            table[row, region] = value
        return carry

    def fill(region, carry):
        block = adj[table[0, region], pl.ds(pl.multiple_of((p.at["x"] * 2 + parity) * rows, rows), rows)]
        asend[region] = jnp.where(table[1, region] == 1, block, jnp.zeros_like(block))
        return carry

    def forward(t):
        pre_f = dot(x_ref[t], wf[0], (1, 0))
        pre_g = dot(x_ref[t], wg[0], (1, 0))
        if t == 1:
            pre_f = pre_f + dot(x_ref[0], wf[1], (1, 0))
            pre_g = pre_g + dot(x_ref[0], wg[1], (1, 0))
        filt = jnp.tanh(pre_f)
        gate = jax.nn.sigmoid(pre_g)
        both = filt * gate
        hid[t] = both.astype(BF16)
        hid_t[t] = hid[t].T
        x_t[t] = x_ref[t].T
        f1[t] = gate * (1.0 - filt * filt)
        f2[t] = both * (1.0 - gate)

    def own_products():
        wm_t[...] = wm[1].T
        for t in range(2):
            cot = gall[t, p.region]
            direct[t] = dot(cot, wm[0], (1, 1))
            here = dot(hid_t[t], cot, (1, 0))
            part[0] = here if t == 0 else part[0] + here

    def send_adjacency():
        arecv[p.region] = asend[p.region]
        for i in range(1, R):
            target = lax.rem(p.region + i, R)
            remote(asend.at[target], arecv.at[p.region], adj_send.at[i], adj_recv.at[i], (p.dp, target))

    def pair_adjacency():
        for i in range(1, R):
            source = lax.rem(p.region + R - i, R)
            arrived(arecv.at[source], adj_send.at[i], adj_recv.at[i])
        remote(arecv, apair, adj_send.at[R], adj_recv.at[R], p.along("y", 1 + (Y - 2) * parity))
        spread(arecv, parity, R)
        afull[p.at["x"], parity] = arecv[...]

    def spread(block, half, base):
        for i in range(1, X):
            remote(block, afull.at[p.at["x"], half], adj_send.at[base + i], adj_recv.at[base + i], p.along("x", i))

    def share_adjacency():
        arrived(apair, adj_send.at[R], adj_recv.at[R])
        spread(apair, 1 - parity, R + X)
        afull[p.at["x"], 1 - parity] = apair[...]

    def wait_adjacency():
        for half, base in ((parity, R), (1 - parity, R + X)):
            for i in range(1, X):
                source = lax.rem(p.at["x"] + X - i, X)
                arrived(afull.at[source, half], adj_send.at[base + i], adj_recv.at[base + i])

    def build(chip, carry):
        for core in range(2):
            region = chip * 2 + core
            block = afull[:, :, region].reshape(TILE, TILE).T
            zero = jnp.zeros_like(block)
            for j in range(2):
                bmat[chip, j * TILE:(j + 1) * TILE, core * TILE:(core + 1) * TILE] = jnp.where(
                    table[3, region] == j, block, zero)
        return carry

    def gathered(step):
        for t in range(2):
            for direction in range(2):
                if step > (Z // 2 if t == direction else Z // 2 - 1) or (step == 0 and direction == 1):
                    continue
                chip = origin(direction, step)
                for tile in range(2):
                    arrived(gall.at[t, chip * 2 + 1 - p.c, pl.ds(tile * TILE, TILE)],
                            sib_send.at[direction, t, step, tile], sib_recv.at[direction, t, step, tile])
                halves = []
                for core in range(2):
                    region = chip * 2 + core
                    halves.append(jnp.where(table[2, region] == 0, gall[t, region, :TILE], gall[t, region, TILE:]))
                more = dot(bmat[chip], jnp.concatenate(halves, axis=0), (1, 0))
                acc[t] = more if step == 0 else acc[t] + more

    for item in get_cot:
        item.wait()
    pl.semaphore_wait(barrier, len(partners))
    ring(0)
    lax.fori_loop(0, R, scan, 0)
    get_adj.wait()
    lax.fori_loop(0, R, fill, 0)
    send_adjacency()
    for item in (get_x, get_wf, get_wg):
        item.wait()
    forward(0)
    ring(1, (0,))
    forward(1)
    ring(1, (1,))
    pair_adjacency()
    ring(2, (0,))
    share_adjacency()
    get_wm.wait()
    own_products()
    ring(2, (1,))
    for step in range(3, Z // 2):
        ring(step, (0,))
        ring(step, (1,))
    wait_adjacency()
    lax.fori_loop(0, Z, build, 0)
    for step in range(Z // 2 - 1):
        gathered(step)
    if Z > 4:
        ring(Z // 2)
    gathered(Z // 2 - 1)
    gathered(Z // 2)

    def settle(items):
        for item in items:
            item.wait_send()

    def taken():
        items = list(sends)
        sends.clear()
        return items

    before = taken()
    groups = [
        Reduction(p, order, part, 2 * i, factor, scratch[i], sems[i], sends) for i, order in enumerate(ORDERS)
    ]
    mixed = [acc[t].astype(BF16) for t in range(2)]
    part[1] = dot(hid_t[0], mixed[0], (1, 0)) + dot(hid_t[1], mixed[1], (1, 0))
    groups[0].start_core()
    for t in range(2):
        grad = direct[t] + dot(mixed[t], wm_t[...], (1, 0))
        actcot[0, t] = (grad * f1[t]).astype(BF16)
        actcot[1, t] = (grad * f2[t]).astype(BF16)
    for g in range(2):
        part[2 + 2 * g] = dot(x_t[0], actcot[g, 0], (1, 0)) + dot(x_t[1], actcot[g, 1], (1, 0))
        part[3 + 2 * g] = dot(x_t[0], actcot[g, 1], (1, 0))
        groups[1 + g].start_core()
        groups[g].start_first()
    groups[2].start_first()
    late, also, early = groups
    for t in range(2):
        total = gall[t, p.region].astype(F32)
        for tap in range(2 - t):
            total = total + dot(actcot[0, t + tap], wf[tap], (1, 1)) + dot(actcot[1, t + tap], wg[tap], (1, 1))
        gi_vmem[t] = total.astype(BF16)
    puts = [pltpu.make_async_copy(gi_vmem, gi_ref, local_sem.at[7])]
    puts[0].start()
    settle(before)
    stages = [
        (name, (early, late, also)) for name in ("start_second", "start_third", "start_gather_second")
    ] + [("start_gather_first", (late, also, early)), ("start_gather_core", (early, late, also))]
    for name, order in stages:
        before = taken()
        for group in order:
            getattr(group, name)()
        settle(before)
    outs = [out_mix, out_filter, out_gate]
    for group in (early, late, also):
        puts += group.put(outs[groups.index(group)], put_sem, 0)
    for group in (early, late, also):
        group.wait()
        puts += group.put(outs[groups.index(group)], put_sem, 1)
    settle(sends)
    for item in puts:
        item.wait()


def write(gi, mix, filt, gate, gi_out, mix_out, filt_out, gate_out, gi_vmem, narrow, wide, sem):
    gets = [pltpu.make_async_copy(ref, narrow.at[i], sem.at[i]) for i, ref in enumerate((mix, filt, gate))]
    gets.append(pltpu.make_async_copy(gi, gi_vmem, sem.at[3]))
    for item in gets:
        item.start()
    puts = [pltpu.make_async_copy(wide.at[i], ref, sem.at[4 + i]) for i, ref in enumerate((mix_out, filt_out, gate_out))]
    puts.append(pltpu.make_async_copy(gi_vmem, gi_out, sem.at[7]))
    for i in range(4):
        gets[i].wait()
        if i < 3:
            wide[i] = narrow[i].astype(F32)
        puts[i].start()
    for item in puts:
        item.wait()


def reduction_scratch(order, chans, sizes):
    n1, n2, n3 = (sizes[axis] for axis in order)
    each = 2 * (TILE // n1 // 8) * (chans // 128) // n2
    return [
        pltpu.VMEM((2, TILE, chans), F32),
        pltpu.VMEM((n1, 2, TILE // n1, chans), BF16),
        pltpu.VMEM((n1 - 1, 2, TILE // n1, chans), BF16),
        pltpu.VMEM((n2, each, 8, 128), F32),
        pltpu.VMEM((n2 - 1, each, 8, 128), F32),
        pltpu.VMEM((n3, each, 8, 128), F32),
        pltpu.VMEM((n2, each, 8, 128), F32),
        pltpu.VMEM((n1, 2, TILE // n1, chans), BF16),
        pltpu.VMEM((n1, 2, TILE // n1, chans), BF16),
    ]


def solution(mesh):
    Y, Z = mesh.shape["dp"] // X, mesh.shape["region"] // 2
    R = 2 * Z
    sizes = {"x": X, "y": Y, "z": Z}

    def per_device(inputs, cotangent, w_filter, w_gate, w_mix, neighbours, adjacency):
        _, steps, sites, chans = inputs.shape
        total_rows = steps * sites * mesh.shape["dp"] * R
        per_tile = neighbours.shape[1]
        dma = pltpu.SemaphoreType.DMA
        vmem = pl.BlockSpec(memory_space=pltpu.VMEM)
        hbm = pl.BlockSpec(memory_space=pltpu.HBM)
        scratch, sems = [], []
        for order in ORDERS:
            scratch += reduction_scratch(order, chans, sizes)
            n1, n2, n3 = (sizes[axis] for axis in order)
            count = 2 + 2 * (n1 - 1) + 2 * (n2 - 1) + n3 - 1
            sems += [dma((count,)), dma((count,))]
        weights = pltpu.VMEM((2, chans, chans), BF16)
        wide = pltpu.VMEM((steps, sites, chans), F32)
        narrow = pltpu.VMEM((steps, sites, chans), BF16)
        shapes = [(2, 2, sizes[order[0]], TILE // sizes[order[0]], chans) for order in ORDERS]
        grad_inputs, *grads = pl.pallas_call(
            functools.partial(kernel, Y, Z, 1.0 / math.sqrt(total_rows)),
            out_shape=[
                jax.ShapeDtypeStruct(shape, BF16) for shape in [(steps, sites, chans), *shapes]
            ],
            in_specs=[pl.BlockSpec(memory_space=pltpu.SMEM)] + [hbm] * 6,
            out_specs=[hbm] * 4,
            scratch_shapes=[
                narrow, dma((2, 6)), narrow, weights, weights, weights,
                pltpu.VMEM((2 * per_tile, TILE, TILE), BF16),
                pltpu.VMEM((steps, R, sites, chans), BF16),
                *[pltpu.VMEM((R, TILE // (2 * X), TILE), BF16)] * 3,
                pltpu.VMEM((X, 2, R, TILE // (2 * X), TILE), BF16),
                pltpu.VMEM((Z, 2 * TILE, 2 * TILE), BF16),
                wide, wide, narrow, narrow, narrow, pltpu.VMEM((chans, chans), BF16), wide, wide,
                pltpu.VMEM((2, steps, sites, chans), BF16),
                pltpu.VMEM((6, chans, chans), F32),
                pltpu.SMEM((4, R), jnp.int32),
                *scratch,
                dma((8,)),
                dma((2, 2, Z // 2, 2)), dma((2, 2, Z // 2, 2)),
                dma((2, 2, Z // 2 + 1, 2)), dma((2, 2, Z // 2 + 1, 2)),
                dma((R + 2 * X,)), dma((R + 2 * X,)),
                *sems,
            ],
            compiler_params=pltpu.CompilerParams(
                collective_id=0, has_side_effects=True, vmem_limit_bytes=56 << 20),
            name="train_step",
        )(neighbours.T, inputs[0], cotangent[0], w_filter, w_gate, w_mix,
          adjacency.reshape(2 * per_tile, TILE, TILE))
        grad = jax.ShapeDtypeStruct((2, chans, chans), F32)
        grad_inputs, grad_mix, grad_filter, grad_gate = pl.pallas_call(
            write,
            out_shape=(jax.ShapeDtypeStruct((steps, sites, chans), BF16), grad, grad, grad),
            in_specs=[hbm] * 4,
            out_specs=(hbm,) * 4,
            scratch_shapes=[
                narrow, pltpu.VMEM((3, 2, chans, chans), BF16), pltpu.VMEM((3, 2, chans, chans), F32), dma((8,)),
            ],
            name="write",
        )(grad_inputs, *[block.reshape(2, chans, chans) for block in grads])
        return grad_inputs[None], grad_filter, grad_gate, grad_mix

    return jax.shard_map(
        per_device,
        mesh=mesh,
        in_specs=(
            P("dp", None, "region", None),
            P("dp", None, "region", None),
            P(),
            P(),
            P(),
            P(),
            P("region", None, None, None),
        ),
        out_specs=(P("dp", None, "region", None), P(), P(), P()),
        check_vma=False,
    )
```

```python
import functools
import itertools
import math

import jax
import jax.numpy as jnp
from jax import lax
from jax.experimental import pallas as pl
from jax.experimental.pallas import tpu as pltpu
from jax.sharding import PartitionSpec as P

MESH = pl.DeviceIdType.MESH
X = 4
TILE = 128
ORDERS = ("yxz", "zxy", "xzy")
F32 = jnp.float32
BF16 = jnp.bfloat16


def dot(a, b, contract):
    return lax.dot_general(a, b, ((contract[:1], contract[1:]), ((), ())), preferred_element_type=F32)


class Place:
    def __init__(self, Y, Z):
        self.size = {"x": X, "y": Y, "z": Z}
        self.dp = lax.axis_index("dp")
        self.region = lax.axis_index("region")
        self.at = {
            "x": lax.div(self.dp, Y), "y": lax.rem(self.dp, Y), "z": lax.div(self.region, 2),
        }
        self.c = lax.rem(self.region, 2)
        self.sibling = (self.dp, self.at["z"] * 2 + 1 - self.c)

    def along(self, axis, i):
        at = dict(self.at)
        at[axis] = lax.rem(at[axis] + i, self.size[axis])
        return (at["x"] * self.size["y"] + at["y"], at["z"] * 2 + self.c)


class Reduction:
    def __init__(self, place, order, part, base, factor, scratch, sems, sends):
        self.p, self.order, self.part, self.base, self.factor, self.sends = place, order, part, base, factor, sends
        self.core, self.s1, self.r1, self.s2, self.r2, self.x3, self.g2, self.g1, self.cg = scratch
        self.send, self.recv = sems
        self.items, self.used = [], 0

    def copy(self, src, dst, device):
        item = pltpu.make_async_remote_copy(
            src_ref=src, dst_ref=dst, send_sem=self.send.at[self.used], recv_sem=self.recv.at[self.used],
            device_id=device, device_id_type=MESH,
        )
        self.used += 1
        item.start()
        self.sends.append(item)
        self.items.append(item)

    def wait(self):
        for item in self.items:
            item.wait_recv()
        self.items = []

    def peers(self, k):
        axis = self.order[k]
        n, at = self.p.size[axis], self.p.at[axis]
        return n, at, [(i, lax.rem(at + i, n), self.p.along(axis, i)) for i in range(1, n)]

    def start_core(self):
        other = pl.ds(pl.multiple_of((1 - self.p.c) * TILE, TILE), TILE)
        self.copy(self.part.at[pl.ds(self.base, 2), other], self.core, self.p.sibling)

    def start_first(self):
        self.wait()
        n, at, peers = self.peers(0)
        mine = pl.ds(pl.multiple_of(self.p.c * TILE, TILE), TILE)
        for i in range(2):
            total = self.core[i] + self.part[self.base + i, mine]
            self.core[i] = total
            self.s1[:, i] = total.astype(BF16).reshape(n, TILE // n, total.shape[-1])
        for i, slot, device in peers:
            self.copy(self.s1.at[slot], self.r1.at[i - 1], device)

    def start_second(self):
        self.wait()
        first, at, _ = self.peers(0)
        rows = TILE // first
        tiles = []
        for i in range(2):
            total = self.core[i, pl.ds(pl.multiple_of(at * rows, rows), rows)]
            for j in range(first - 1):
                total = total + self.r1[j, i].astype(F32)
            tiles += [
                total[r * 8:r * 8 + 8, h * 128:h * 128 + 128] for r in range(rows // 8) for h in range(2)
            ]
        n, at, peers = self.peers(1)
        each = len(tiles) // n
        for index, tile in enumerate(tiles):
            self.s2[index // each, index % each] = tile
        for i, slot, device in peers:
            self.copy(self.s2.at[slot], self.r2.at[i - 1], device)

    def start_third(self):
        self.wait()
        n, at, _ = self.peers(1)
        total = self.s2[at]
        for j in range(n - 1):
            total = total + self.r2[j]
        n, at, peers = self.peers(2)
        self.x3[at] = total
        for i, slot, device in peers:
            self.copy(self.x3.at[at], self.x3.at[at], device)

    def start_gather_second(self):
        self.wait()
        total = self.x3[0]
        for j in range(1, self.peers(2)[0]):
            total = total + self.x3[j]
        n, at, peers = self.peers(1)
        self.g2[at] = total * self.factor
        for i, slot, device in peers:
            self.copy(self.g2.at[at], self.g2.at[at], device)

    def start_gather_first(self):
        self.wait()
        n, at, peers = self.peers(0)
        each = self.g2.shape[1]
        tiles = [self.g2[i, j] for i in range(self.g2.shape[0]) for j in range(each)]
        for i in range(2):
            mine = tiles[i * len(tiles) // 2:(i + 1) * len(tiles) // 2]
            rows = [jnp.concatenate(mine[r:r + 2], axis=1) for r in range(0, len(mine), 2)]
            self.g1[at, i] = jnp.concatenate(rows, axis=0).astype(BF16)
        for i, slot, device in peers:
            self.copy(self.g1.at[at], self.g1.at[at], device)
        self.gathered, self.items = self.items, []
        self.copy(self.g1.at[at], self.cg.at[at], self.p.sibling)

    def start_gather_core(self):
        n, at, _ = self.peers(0)
        for i, item in enumerate(self.gathered, 1):
            item.wait_recv()
            slot = lax.rem(at + n - i, n)
            self.copy(self.g1.at[slot], self.cg.at[slot], self.p.sibling)

    def put(self, out, sem, other):
        source, core = (self.cg, 1 - self.p.c) if other else (self.g1, self.p.c)
        copies = [
            pltpu.make_async_copy(source.at[:, i], out.at[i, core], sem.at[other, self.base + i]) for i in range(2)
        ]
        for item in copies:
            item.start()
        return copies


def kernel(Y, Z, factor, nbr, x_hbm, cot_hbm, wf_hbm, wg_hbm, wm_hbm, adj_hbm,
           gi_ref, out_mix, out_filter, out_gate,
           gi_vmem, put_sem, x_ref, wf, wg, wm, adj, gall, asend, arecv, apair, afull, bmat, direct, acc, hid, hid_t, x_t, wm_t, f1, f2, actcot, part, table,
           *rest):
    scratch = [rest[9 * i:9 * i + 9] for i in range(3)]
    local_sem, ring_send, ring_recv, sib_send, sib_recv, adj_send, adj_recv = rest[27:34]
    sems = [rest[34 + 2 * i:36 + 2 * i] for i in range(3)]
    p = Place(Y, Z)
    R = 2 * Z
    per_tile = nbr.shape[0]
    entries = 2 * per_tile
    rows = TILE // (2 * X)
    parity = lax.rem(p.at["y"], 2)
    sends = []

    def fetch(i, src, dst):
        item = pltpu.make_async_copy(src, dst, local_sem.at[i])
        item.start()
        return item

    get_cot = [fetch(t, cot_hbm.at[t], gall.at[t, p.region]) for t in range(2)]
    get_adj = fetch(2, adj_hbm, adj)
    get_x = fetch(3, x_hbm, x_ref)
    get_wf = fetch(4, wf_hbm, wf)
    get_wg = fetch(5, wg_hbm, wg)
    get_wm = fetch(6, wm_hbm, wm)

    barrier = pltpu.get_barrier_semaphore()
    partners = [(p.dp, lax.rem(p.region + i, R)) for i in range(1, R)]
    partners += [p.along(axis, i) for axis, n in (("x", X), ("y", Y)) for i in range(1, n)]
    for device in partners:
        pl.semaphore_signal(barrier, inc=1, device_id=device, device_id_type=MESH)

    def remote(src, dst, send, recv, device):
        item = pltpu.make_async_remote_copy(
            src_ref=src, dst_ref=dst, send_sem=send, recv_sem=recv, device_id=device, device_id_type=MESH)
        item.start()
        sends.append(item)

    def arrived(ref, send, recv):
        pltpu.make_async_remote_copy(
            src_ref=ref, dst_ref=ref, send_sem=send, recv_sem=recv, device_id=p.sibling, device_id_type=MESH
        ).wait_recv()

    def origin(direction, step):
        return lax.rem(p.at["z"] + (Z - step if direction == 0 else step), Z)

    def ring(step, times=(0, 1)):
        for t, tile, direction in itertools.product(times, range(2), range(2)):
            reach = Z // 2 if t == direction else Z // 2 - 1
            if step > reach:
                continue
            block = gall.at[t, origin(direction, step) * 2 + p.c, pl.ds(tile * TILE, TILE)]
            if step > 0:
                arrived(block, ring_send.at[direction, t, step - 1, tile], ring_recv.at[direction, t, step - 1, tile])
            if step < reach:
                remote(block, block, ring_send.at[direction, t, step, tile], ring_recv.at[direction, t, step, tile],
                       p.along("z", 1 if direction == 0 else Z - 1))
            if step > 0 or direction == 0:
                remote(block, block, sib_send.at[direction, t, step, tile], sib_recv.at[direction, t, step, tile],
                       p.sibling)

    def scan(region, carry):
        entry = valid = other = mine = jnp.int32(0)
        for e in range(entries):
            a = nbr[e % per_tile, p.region * 2 + e // per_tile]
            hit = lax.div(a, 2) == region
            entry = jnp.where(hit, e, entry)
            valid = jnp.where(hit, 1, valid)
            b = nbr[e % per_tile, region * 2 + e // per_tile]
            back = lax.div(b, 2) == p.region
            other = jnp.where(back, e // per_tile, other)
            mine = jnp.where(back, lax.rem(b, 2), mine)
        for row, value in enumerate((entry, valid, other, mine)):
            table[row, region] = value
        return carry

    def fill(region, carry):
        block = adj[table[0, region], pl.ds(pl.multiple_of((p.at["x"] * 2 + parity) * rows, rows), rows)]
        asend[region] = jnp.where(table[1, region] == 1, block, jnp.zeros_like(block))
        return carry

    def forward(t):
        pre_f = dot(x_ref[t], wf[0], (1, 0))
        pre_g = dot(x_ref[t], wg[0], (1, 0))
        if t == 1:
            pre_f = pre_f + dot(x_ref[0], wf[1], (1, 0))
            pre_g = pre_g + dot(x_ref[0], wg[1], (1, 0))
        filt = jnp.tanh(pre_f)
        gate = jax.nn.sigmoid(pre_g)
        both = filt * gate
        hid[t] = both.astype(BF16)
        hid_t[t] = hid[t].T
        x_t[t] = x_ref[t].T
        f1[t] = gate * (1.0 - filt * filt)
        f2[t] = both * (1.0 - gate)

    def own_products():
        wm_t[...] = wm[1].T
        for t in range(2):
            cot = gall[t, p.region]
            direct[t] = dot(cot, wm[0], (1, 1))
            here = dot(hid_t[t], cot, (1, 0))
            part[0] = here if t == 0 else part[0] + here

    def send_adjacency():
        arecv[p.region] = asend[p.region]
        for i in range(1, R):
            target = lax.rem(p.region + i, R)
            remote(asend.at[target], arecv.at[p.region], adj_send.at[i], adj_recv.at[i], (p.dp, target))

    def pair_adjacency():
        for i in range(1, R):
            source = lax.rem(p.region + R - i, R)
            arrived(arecv.at[source], adj_send.at[i], adj_recv.at[i])
        remote(arecv, apair, adj_send.at[R], adj_recv.at[R], p.along("y", 1 + (Y - 2) * parity))
        spread(arecv, parity, R)
        afull[p.at["x"], parity] = arecv[...]

    def spread(block, half, base):
        for i in range(1, X):
            remote(block, afull.at[p.at["x"], half], adj_send.at[base + i], adj_recv.at[base + i], p.along("x", i))

    def share_adjacency():
        arrived(apair, adj_send.at[R], adj_recv.at[R])
        spread(apair, 1 - parity, R + X)
        afull[p.at["x"], 1 - parity] = apair[...]

    def wait_adjacency():
        for half, base in ((parity, R), (1 - parity, R + X)):
            for i in range(1, X):
                source = lax.rem(p.at["x"] + X - i, X)
                arrived(afull.at[source, half], adj_send.at[base + i], adj_recv.at[base + i])

    def build(chip, carry):
        for core in range(2):
            region = chip * 2 + core
            block = afull[:, :, region].reshape(TILE, TILE).T
            zero = jnp.zeros_like(block)
            for j in range(2):
                bmat[chip, j * TILE:(j + 1) * TILE, core * TILE:(core + 1) * TILE] = jnp.where(
                    table[3, region] == j, block, zero)
        return carry

    def gathered(step):
        for t in range(2):
            for direction in range(2):
                if step > (Z // 2 if t == direction else Z // 2 - 1) or (step == 0 and direction == 1):
                    continue
                chip = origin(direction, step)
                for tile in range(2):
                    arrived(gall.at[t, chip * 2 + 1 - p.c, pl.ds(tile * TILE, TILE)],
                            sib_send.at[direction, t, step, tile], sib_recv.at[direction, t, step, tile])
                halves = []
                for core in range(2):
                    region = chip * 2 + core
                    halves.append(jnp.where(table[2, region] == 0, gall[t, region, :TILE], gall[t, region, TILE:]))
                more = dot(bmat[chip], jnp.concatenate(halves, axis=0), (1, 0))
                acc[t] = more if step == 0 else acc[t] + more

    for item in get_cot:
        item.wait()
    pl.semaphore_wait(barrier, len(partners))
    ring(0)
    lax.fori_loop(0, R, scan, 0)
    get_adj.wait()
    lax.fori_loop(0, R, fill, 0)
    send_adjacency()
    for item in (get_x, get_wf, get_wg):
        item.wait()
    forward(0)
    ring(1, (0,))
    forward(1)
    ring(1, (1,))
    pair_adjacency()
    ring(2, (0,))
    share_adjacency()
    get_wm.wait()
    own_products()
    ring(2, (1,))
    for step in range(3, Z // 2):
        ring(step, (0,))
        ring(step, (1,))
    wait_adjacency()
    lax.fori_loop(0, Z, build, 0)
    for step in range(Z // 2 - 1):
        gathered(step)
    if Z > 4:
        ring(Z // 2)
    gathered(Z // 2 - 1)
    gathered(Z // 2)

    def settle(items):
        for item in items:
            item.wait_send()

    def taken():
        items = list(sends)
        sends.clear()
        return items

    before = taken()
    groups = [
        Reduction(p, order, part, 2 * i, factor, scratch[i], sems[i], sends) for i, order in enumerate(ORDERS)
    ]
    mixed = [acc[t].astype(BF16) for t in range(2)]
    part[1] = dot(hid_t[0], mixed[0], (1, 0)) + dot(hid_t[1], mixed[1], (1, 0))
    groups[0].start_core()
    for t in range(2):
        grad = direct[t] + dot(mixed[t], wm_t[...], (1, 0))
        actcot[0, t] = (grad * f1[t]).astype(BF16)
        actcot[1, t] = (grad * f2[t]).astype(BF16)
    for g in range(2):
        part[2 + 2 * g] = dot(x_t[0], actcot[g, 0], (1, 0)) + dot(x_t[1], actcot[g, 1], (1, 0))
        part[3 + 2 * g] = dot(x_t[0], actcot[g, 1], (1, 0))
        groups[1 + g].start_core()
        groups[g].start_first()
    groups[2].start_first()
    late, also, early = groups
    for t in range(2):
        total = gall[t, p.region].astype(F32)
        for tap in range(2 - t):
            total = total + dot(actcot[0, t + tap], wf[tap], (1, 1)) + dot(actcot[1, t + tap], wg[tap], (1, 1))
        gi_vmem[t] = total.astype(BF16)
    puts = [pltpu.make_async_copy(gi_vmem, gi_ref, local_sem.at[7])]
    puts[0].start()
    settle(before)
    stages = [
        (name, (early, late, also)) for name in ("start_second", "start_third", "start_gather_second")
    ] + [("start_gather_first", (late, also, early)), ("start_gather_core", (early, late, also))]
    for name, order in stages:
        before = taken()
        for group in order:
            getattr(group, name)()
        settle(before)
    outs = [out_mix, out_filter, out_gate]
    for group in (early, late, also):
        puts += group.put(outs[groups.index(group)], put_sem, 0)
    for group in (early, late, also):
        group.wait()
        puts += group.put(outs[groups.index(group)], put_sem, 1)
    settle(sends)
    for item in puts:
        item.wait()


def write(gi, mix, filt, gate, gi_out, mix_out, filt_out, gate_out, gi_vmem, narrow, wide, sem):
    gets = [pltpu.make_async_copy(ref, narrow.at[i], sem.at[i]) for i, ref in enumerate((mix, filt, gate))]
    gets.append(pltpu.make_async_copy(gi, gi_vmem, sem.at[3]))
    for item in gets:
        item.start()
    puts = [pltpu.make_async_copy(wide.at[i], ref, sem.at[4 + i]) for i, ref in enumerate((mix_out, filt_out, gate_out))]
    puts.append(pltpu.make_async_copy(gi_vmem, gi_out, sem.at[7]))
    for i in range(4):
        gets[i].wait()
        if i < 3:
            wide[i] = narrow[i].astype(F32)
        puts[i].start()
    for item in puts:
        item.wait()


def reduction_scratch(order, chans, sizes):
    n1, n2, n3 = (sizes[axis] for axis in order)
    each = 2 * (TILE // n1 // 8) * (chans // 128) // n2
    return [
        pltpu.VMEM((2, TILE, chans), F32),
        pltpu.VMEM((n1, 2, TILE // n1, chans), BF16),
        pltpu.VMEM((n1 - 1, 2, TILE // n1, chans), BF16),
        pltpu.VMEM((n2, each, 8, 128), F32),
        pltpu.VMEM((n2 - 1, each, 8, 128), F32),
        pltpu.VMEM((n3, each, 8, 128), F32),
        pltpu.VMEM((n2, each, 8, 128), F32),
        pltpu.VMEM((n1, 2, TILE // n1, chans), BF16),
        pltpu.VMEM((n1, 2, TILE // n1, chans), BF16),
    ]


def solution(mesh):
    Y, Z = mesh.shape["dp"] // X, mesh.shape["region"] // 2
    R = 2 * Z
    sizes = {"x": X, "y": Y, "z": Z}

    def per_device(inputs, cotangent, w_filter, w_gate, w_mix, neighbours, adjacency):
        _, steps, sites, chans = inputs.shape
        total_rows = steps * sites * mesh.shape["dp"] * R
        per_tile = neighbours.shape[1]
        dma = pltpu.SemaphoreType.DMA
        vmem = pl.BlockSpec(memory_space=pltpu.VMEM)
        hbm = pl.BlockSpec(memory_space=pltpu.HBM)
        scratch, sems = [], []
        for order in ORDERS:
            scratch += reduction_scratch(order, chans, sizes)
            n1, n2, n3 = (sizes[axis] for axis in order)
            count = 2 + 3 * (n1 - 1) + 2 * (n2 - 1) + n3 - 1
            sems += [dma((count,)), dma((count,))]
        weights = pltpu.VMEM((2, chans, chans), BF16)
        wide = pltpu.VMEM((steps, sites, chans), F32)
        narrow = pltpu.VMEM((steps, sites, chans), BF16)
        shapes = [(2, 2, sizes[order[0]], TILE // sizes[order[0]], chans) for order in ORDERS]
        grad_inputs, *grads = pl.pallas_call(
            functools.partial(kernel, Y, Z, 1.0 / math.sqrt(total_rows)),
            out_shape=[
                jax.ShapeDtypeStruct(shape, BF16) for shape in [(steps, sites, chans), *shapes]
            ],
            in_specs=[pl.BlockSpec(memory_space=pltpu.SMEM)] + [hbm] * 6,
            out_specs=[hbm] * 4,
            scratch_shapes=[
                narrow, dma((2, 6)), narrow, weights, weights, weights,
                pltpu.VMEM((2 * per_tile, TILE, TILE), BF16),
                pltpu.VMEM((steps, R, sites, chans), BF16),
                *[pltpu.VMEM((R, TILE // (2 * X), TILE), BF16)] * 3,
                pltpu.VMEM((X, 2, R, TILE // (2 * X), TILE), BF16),
                pltpu.VMEM((Z, 2 * TILE, 2 * TILE), BF16),
                wide, wide, narrow, narrow, narrow, pltpu.VMEM((chans, chans), BF16), wide, wide,
                pltpu.VMEM((2, steps, sites, chans), BF16),
                pltpu.VMEM((6, chans, chans), F32),
                pltpu.SMEM((4, R), jnp.int32),
                *scratch,
                dma((8,)),
                dma((2, 2, Z // 2, 2)), dma((2, 2, Z // 2, 2)),
                dma((2, 2, Z // 2 + 1, 2)), dma((2, 2, Z // 2 + 1, 2)),
                dma((R + 2 * X,)), dma((R + 2 * X,)),
                *sems,
            ],
            compiler_params=pltpu.CompilerParams(
                collective_id=0, has_side_effects=True, vmem_limit_bytes=56 << 20),
            name="train_step",
        )(neighbours.T, inputs[0], cotangent[0], w_filter, w_gate, w_mix,
          adjacency.reshape(2 * per_tile, TILE, TILE))
        grad = jax.ShapeDtypeStruct((2, chans, chans), F32)
        grad_inputs, grad_mix, grad_filter, grad_gate = pl.pallas_call(
            write,
            out_shape=(jax.ShapeDtypeStruct((steps, sites, chans), BF16), grad, grad, grad),
            in_specs=[hbm] * 4,
            out_specs=(hbm,) * 4,
            scratch_shapes=[
                narrow, pltpu.VMEM((3, 2, chans, chans), BF16), pltpu.VMEM((3, 2, chans, chans), F32), dma((8,)),
            ],
            name="write",
        )(grad_inputs, *[block.reshape(2, chans, chans) for block in grads])
        return grad_inputs[None], grad_filter, grad_gate, grad_mix

    return jax.shard_map(
        per_device,
        mesh=mesh,
        in_specs=(
            P("dp", None, "region", None),
            P("dp", None, "region", None),
            P(),
            P(),
            P(),
            P(),
            P("region", None, None, None),
        ),
        out_specs=(P("dp", None, "region", None), P(), P(), P()),
        check_vma=False,
    )
```
